512 devices in a mesh: wide: 32 (over y, x), narrow: 16 (over z, core).
Axes of the slice: x: 4, y: 8, z: 8, core: 2. Of those that a mesh axis runs over, the one named last changes fastest.
Arguments:
- blocks: float32 [32, 16, 2, 64, 4096], P('wide', 'narrow'), may hold values from -786432 to 786432
- block_coords: int32 [32, 16, 2, 3], P('wide', 'narrow'), may hold values from 0 to 63, as said below
- block_count: int32 [32, 16], P('wide', 'narrow'), may hold values from 0 to 2, as said below
- orbital_factor: float32 [4096, 128], P('narrow'), may hold values from -8 to 8
Outputs:
- aux_new: float32 [16, 1024, 128], P('narrow', 'wide')
- orbital_new: float32 [4096, 128], P('narrow')
The draws below stay inside these ranges and needn't reach their ends.
Inputs may be any that keep to these rules, and one draw needn't show every extreme that they name: `block_coords`: entries are (auxiliary block 0 to 15, orbital block 0 to 63, orbital block 0 to 63); no triple repeats within a column. `block_count`: slot s of a device is live when s < its count; some device holds 2 live blocks in every draw.
All inputs are finite; a program needn't handle non-finite values.
Results may differ from the reference program's by a relative error of at most 0.0003.
Values sent between devices are 32-bit elements; how exact they have to be, the bound alone decides.
A program may use at most 64 MiB of HBM per device.

```python
import jax
import jax.numpy as jnp
from jax import lax

R = 128
E = 64
NP = 16384
NO = 4096
SLOTS = 2
WIDES = 32
COLS = 16
QB = 16
OB = 64


def draw_block_coords(key, part):
    column_keys = jax.random.split(jax.random.fold_in(key, 11), COLS)

    def one_column(column_key):
        chosen = jax.random.permutation(column_key, QB * OB * OB)[:WIDES * SLOTS]
        aux_block = chosen // (OB * OB)
        first_orb = chosen // OB % OB
        second_orb = chosen % OB
        return jnp.stack([aux_block, first_orb, second_orb], axis=-1).reshape(WIDES, SLOTS, 3)
    columns = jax.vmap(one_column)(column_keys)
    return jnp.transpose(columns, (1, 0, 2, 3)).astype(jnp.int32)


def draw_block_count(key, part):
    count_key, full_key = jax.random.split(jax.random.fold_in(key, 23))
    counts = jax.random.randint(count_key, (WIDES * COLS,), 0, SLOTS + 1)
    full_device = jax.random.randint(full_key, (), 0, WIDES * COLS)
    counts = jnp.where(jnp.arange(WIDES * COLS) == full_device, SLOTS, counts)
    return counts.reshape(WIDES, COLS).astype(jnp.int32)


def draw_orbital_factor(key, part):
    noise_key, mean_key, shape_key = jax.random.split(jax.random.fold_in(key, 37), 3)
    noise = jax.random.normal(noise_key, (NO, R), jnp.float32)
    common = jax.random.normal(mean_key, (NO, 1), jnp.float32)
    profile = jax.random.uniform(shape_key, (1, R), jnp.float32, 0.5, 1.5)
    return jnp.clip(noise + common * profile, -8.0, 8.0).astype(jnp.float32)


def levels(rng, extent, cuts, least, high):
    def one(axis_at, blocks):
        heights = jax.random.uniform(jax.random.fold_in(jax.random.fold_in(rng, 6), axis_at), (blocks,), jnp.float32, least / len(cuts), high / len(cuts))
        return jnp.repeat(jnp.exp(heights), extent[axis_at] // blocks).reshape((-1,) + (1,) * (len(extent) - axis_at - 1))

    level = one(*cuts[0])
    for cut in cuts[1:]:
        level = level * one(*cut)
    return level


def gaussian(own_key, extent, scale, reach, cuts=(), held_as=jnp.bfloat16):
    level = levels(own_key, extent, cuts, -0.22, 0.18) if cuts else 1.0
    result = jax.random.normal(own_key, extent, jnp.float32) * scale * level
    return jnp.minimum(jnp.maximum(result, -reach), reach).astype(held_as)


def setup_inputs(seed: int = 0) -> dict:
    key_of = jax.random.split(jax.random.key(seed), 5)
    blocks = gaussian(key_of[0], (WIDES, COLS, SLOTS, E, E * E), (NO * NO // 128), 786432.0, ((0, 32), (1, 16)), jnp.float32)
    block_coords = draw_block_coords(jax.random.fold_in(key_of[4], 71), 0)
    block_count = draw_block_count(jax.random.fold_in(key_of[4], 71), 0)
    orbital_factor = draw_orbital_factor(jax.random.fold_in(key_of[4], 71), 0)
    return {"blocks": blocks, "block_coords": block_coords, "block_count": block_count, "orbital_factor": orbital_factor}


precise_level = lax.Precision.HIGHEST

def product(left, right):
    return jnp.dot(left.astype(jnp.float32), right.astype(jnp.float32), precision=precise_level, preferred_element_type=jnp.float32)

def inverse_of(gram):
    lower = jnp.linalg.cholesky(gram)
    return jax.scipy.linalg.cho_solve((lower, True), jnp.eye(gram.shape[0], dtype=gram.dtype))

def first_mode(tensor_block, rows_i, rows_j):
    block_edge = rows_i.shape[0]
    contracted = product(tensor_block.reshape(block_edge * block_edge, block_edge), rows_j)
    contracted = contracted.reshape(block_edge, block_edge, -1)
    return (contracted, jnp.sum(contracted * rows_i[None], axis=1))

def second_mode(tensor_block, contracted, aux_rows, rows_i):
    block_edge = rows_i.shape[0]
    term_i = jnp.sum(contracted * aux_rows[:, None, :], axis=0)
    spread = product(aux_rows.T, tensor_block).reshape(-1, block_edge, block_edge)
    term_j = jnp.einsum('rij,ir->jr', spread, rows_i, precision=precise_level)
    return (term_i, term_j)

def pick_rows(matrix, index, length):
    return lax.dynamic_slice_in_dim(matrix, (index * length).astype(jnp.int32), length, 0)

def add_rows(total, start, addend):
    current = lax.dynamic_slice_in_dim(total, start.astype(jnp.int32), addend.shape[0], 0)
    return lax.dynamic_update_slice_in_dim(total, current + addend, start.astype(jnp.int32), 0)

def reference(blocks, block_coords, block_count, orbital_factor):
    wide_count, column_count, slot_count, block_edge = (blocks.shape[0], blocks.shape[1], blocks.shape[2], blocks.shape[3])
    factor_rank = orbital_factor.shape[1]
    column_rows = NP // column_count
    flat_blocks = blocks.reshape(-1, block_edge, block_edge * block_edge)
    flat_coords = block_coords.reshape(-1, 3)
    slot_ids = jnp.arange(slot_count, dtype=jnp.int32)
    weights = (slot_ids[None, None, :] < block_count[:, :, None]).astype(jnp.float32).reshape(-1)
    column_ids = jnp.broadcast_to(jnp.arange(column_count, dtype=jnp.int32)[None, :, None], (wide_count, column_count, slot_count)).reshape(-1)
    gram_b = product(orbital_factor.T, orbital_factor)

    def add_aux(total, item):
        tensor_block, coord, weight, column = item
        rows_i = pick_rows(orbital_factor, coord[1], block_edge)
        rows_j = pick_rows(orbital_factor, coord[2], block_edge)
        unused, aux_term = first_mode(tensor_block, rows_i, rows_j)
        start = column * column_rows + coord[0] * block_edge
        return (add_rows(total, start, weight * aux_term), None)
    aux_sum, unused = lax.scan(add_aux, jnp.zeros((NP, factor_rank), jnp.float32), (flat_blocks, flat_coords, weights, column_ids))
    aux_flat = product(aux_sum, inverse_of(gram_b * gram_b))
    gram_a = product(aux_flat.T, aux_flat)

    def add_orbital(total, item):
        tensor_block, coord, weight, column = item
        rows_i = pick_rows(orbital_factor, coord[1], block_edge)
        rows_j = pick_rows(orbital_factor, coord[2], block_edge)
        contracted, unused = first_mode(tensor_block, rows_i, rows_j)
        start = column * column_rows + coord[0] * block_edge
        aux_rows = lax.dynamic_slice_in_dim(aux_flat, start.astype(jnp.int32), block_edge, 0)
        term_i, term_j = second_mode(tensor_block, contracted, aux_rows, rows_i)
        total = add_rows(total, coord[1] * block_edge, weight * term_i)
        total = add_rows(total, coord[2] * block_edge, weight * term_j)
        return (total, None)
    orbital_sum, unused = lax.scan(add_orbital, jnp.zeros((NO, factor_rank), jnp.float32), (flat_blocks, flat_coords, weights, column_ids))
    orbital_new = product(orbital_sum, inverse_of(2.0 * gram_a * gram_b))
    return (aux_flat.reshape(column_count, column_rows, factor_rank), orbital_new)
```

```python
import functools
import types

import jax
import jax.numpy as jnp
from jax import lax
from jax.experimental import pallas as pl
from jax.experimental.pallas import tpu as pltpu
from jax.sharding import PartitionSpec as P

NX, NY = 4, 8
NW = NX * NY
EDGE = 64
RANK = 128
HALVES = EDGE // NW
QB = 16
SPAN = EDGE * EDGE
CHUNK = 256
SUB = CHUNK // 2
F32, BF16 = jnp.float32, jnp.bfloat16
HIGHEST = lax.Precision.HIGHEST


def dot_full(left, right):
    return jnp.dot(left, right, precision=HIGHEST, preferred_element_type=F32)


def dot_fast(left, right):
    return jnp.dot(left, right, preferred_element_type=F32)


def pivot_step(rows):
    lane = lax.broadcasted_iota(jnp.int32, (8, RANK), 1)
    sub = lax.broadcasted_iota(jnp.int32, (8, RANK), 0)
    head = lane < 8

    def over_lanes(block, column):
        return jnp.broadcast_to(block[:, column : column + 1], (8, RANK))

    def over_rows(block, row):
        return jnp.broadcast_to(block[row : row + 1, :], (8, RANK))

    panel = rows[0]
    cols = [over_lanes(panel, m) for m in range(8)]
    for j in range(8):
        scale = 1.0 / over_rows(cols[j], j)
        fresh = []
        for m in range(8):
            if m == j:
                fresh.append(jnp.where(sub == j, scale, -cols[j] * scale))
            else:
                ratio = over_rows(cols[m], j) * scale
                fresh.append(jnp.where(sub == j, ratio, cols[m] - cols[j] * ratio))
        cols = fresh
    panel = jnp.where(head, jnp.where(lane == sub, 1.0, 0.0), panel)
    solved = cols[0] * over_rows(panel, 0)
    for m in range(1, 8):
        solved = solved + cols[m] * over_rows(panel, m)
    spread = [over_rows(solved, m) for m in range(8)]
    out = []
    for row in rows[1:]:
        total = jnp.where(head, 0.0, row)
        for m in range(8):
            total = total - over_lanes(row, m) * spread[m]
        out.append(total)
    out.append(solved)
    return tuple(pltpu.roll(block, RANK - 8, 1) for block in out)


def invert_steps(ref, first, last):
    rows = tuple(ref[8 * k : 8 * k + 8, :] for k in range(16))
    rows = lax.fori_loop(first, last, lambda t, held: pivot_step(held), rows)
    for k in range(16):
        ref[8 * k : 8 * k + 8, :] = rows[k]


def scratch_plan(nz):
    nc = 2 * nz
    vmem = dict(
        xs=((2, EDGE, SPAN), F32),
        xh=((2, EDGE, SPAN), BF16),
        xl=((2, EDGE, SPAN), BF16),
        xt=((2, SPAN, 3 * EDGE), BF16),
        full=((CHUNK * nc, RANK), F32),
        where=((4 * 8 * nz, RANK), F32),
        picks=((4 * EDGE, RANK), F32),
        krh=((SPAN, RANK), BF16),
        krl=((SPAN, RANK), BF16),
        gram=((RANK, RANK), F32),
        gram_in=((RANK, RANK), F32),
        gram_b=((RANK, RANK), F32),
        gram_own=((RANK, RANK), F32),
        gram_a=((RANK, RANK), F32),
        inv=((RANK, RANK), F32),
        meta=((16, RANK), F32),
        meta_x=((16 * NX, RANK), F32),
        metas=((16 * NW, RANK), F32),
        pick_aux_t=((4 * NW, RANK), F32),
        pick_aux=((RANK, 4 * NW), F32),
        pick_orb_t=((8 * NW, RANK), F32),
        pick_orb=((RANK, 8 * NW), F32),
        pick_reply=((8 * NW, RANK), F32),
        terms=((4 * EDGE, RANK), F32),
        fwd=((4 * NW, RANK), F32),
        fwd_mid=((4 * NW, RANK), F32),
        fwd_turn=((4 * NW, RANK), F32),
        fwd_in=((4 * NW, RANK), F32),
        rep=((8 * NW, RANK), F32),
        rep_mid=((8 * NW, RANK), F32),
        rep_turn=((8 * NW, RANK), F32),
        rep_in=((8 * NW, RANK), F32),
        own=((NW, RANK), F32),
        own_mid=((NW, RANK), F32),
        own_turn=((8 * NY, RANK), F32),
        own_in=((8 * NY, RANK), F32),
        tile=((8, RANK), F32),
        tile_core=((8, RANK), F32),
        tile_sum=((8, RANK), F32),
        tile_all=((8, RANK), F32),
        sum_own=((8, RANK), F32),
        tile_z=((8 * nz, RANK), F32),
        tile_y=((8 * NY, RANK), F32),
        tile_x=((8 * NW, RANK), F32),
        orb=((8 * NW, RANK), F32),
        orb_mid=((8 * NW, RANK), F32),
        orb_turn=((8 * NW, RANK), F32),
        orb_in=((8 * NW, RANK), F32),
        dense=((16 * nz, RANK), F32),
        dense_core=((8 * nz, RANK), F32),
        part=((8 * nz, RANK), F32),
        part_z=((8 * nz, RANK), F32),
        sum_y=((8 * NY, RANK), F32),
        sum_x=((8 * NW, RANK), F32),
        final=((8 * NW, RANK), F32),
    )
    sems = dict(
        load=1,
        up=8,
        down=8,
        across=16,
        grams=1,
        meta_sx=NX,
        meta_sy=NY,
        fwd_sx=NX,
        fwd_sy=NY,
        rep_sx=NX,
        rep_sy=NY,
        own_sx=NX,
        own_sy=NY,
        tile_sc=1,
        tile_sz=nz,
        tile_sy=NY,
        tile_sx=NX,
        orb_sx=NX,
        orb_sy=NY,
        dense_sc=1,
        part_sz=nz,
        sum_sy=NY,
        sum_sx=NX,
    )
    return vmem, sems


def kernel(nz, coords, count, b_in, blocks, aux_out, orb_out, *scratch):
    vmem, sems = scratch_plan(nz)
    m = types.SimpleNamespace(**dict(zip(vmem, scratch)))
    rest = scratch[len(vmem) :]
    sent = dict(zip(sems, rest[: len(sems)]))
    got = dict(zip(sems, rest[len(sems) :]))

    w = lax.axis_index("wide")
    c = lax.axis_index("narrow")
    x, y = w % NX, w // NX
    z, core = c // 2, c % 2
    pending = []

    def send(src, dst, name, index, wide=None, narrow=None):
        copy = pltpu.make_async_remote_copy(
            src_ref=src,
            dst_ref=dst,
            send_sem=sent[name].at[index],
            recv_sem=got[name].at[index],
            device_id=(w if wide is None else wide, c if narrow is None else narrow),
            device_id_type=pl.DeviceIdType.MESH,
        )
        copy.start()
        pending.append(copy)
        return copy

    def rows_of(ref, index, size):
        return ref.at[pl.ds(pl.multiple_of(index * size, 8), size)]

    def over_x(name, piece, dst, size):
        copies = []
        for d in range(1, NX):
            peer = (x + d) % NX
            copies.append(send(piece(peer), rows_of(dst, x, size), name, d, wide=y * NX + peer))
        return copies

    def over_y(name, piece, dst, size):
        copies = []
        for d in range(1, NY):
            peer = (y + d) % NY
            copies.append(send(piece(peer), rows_of(dst, y, size), name, d, wide=peer * NX + x))
        return copies

    def over_z(name, piece, dst, size):
        copies = []
        for d in range(1, nz):
            peer = (z + d) % nz
            copies.append(send(piece(peer), rows_of(dst, z, size), name, d, narrow=peer * 2 + core))
        return copies

    def arrived(copies):
        for copy in copies:
            copy.wait_recv()

    def keep(dst, index, size, src, src_index):
        dst[pl.ds(pl.multiple_of(index * size, 8), size), :] = src[
            pl.ds(pl.multiple_of(src_index * size, 8), size), :
        ]

    load = pltpu.make_async_copy(blocks, m.xs, sent["load"].at[0])
    load.start()

    barrier = pltpu.get_barrier_semaphore()
    for d in range(1, NX):
        pl.semaphore_signal(
            barrier, inc=1, device_id=(y * NX + (x + d) % NX, c), device_id_type=pl.DeviceIdType.MESH
        )
    for d in range(1, NY):
        pl.semaphore_signal(
            barrier, inc=1, device_id=((y + d) % NY * NX + x, c), device_id_type=pl.DeviceIdType.MESH
        )
    for d in range(1, nz):
        pl.semaphore_signal(
            barrier, inc=1, device_id=(w, (z + d) % nz * 2 + core), device_id_type=pl.DeviceIdType.MESH
        )
    partner = z * 2 + 1 - core
    pl.semaphore_signal(barrier, inc=1, device_id=(w, partner), device_id_type=pl.DeviceIdType.MESH)

    lane = lax.broadcasted_iota(jnp.int32, (8, RANK), 1)
    row = lax.broadcasted_iota(jnp.int32, (8, RANK), 0)
    live = [jnp.where(count[0, 0] > s, 1.0, 0.0) for s in range(2)]
    low = jnp.zeros((8, RANK), F32)
    high = jnp.zeros((8, RANK), F32)
    for s in range(2):
        for h in range(HALVES):
            hit = (row == 2 * s + h) & (lane == h * QB + coords[s, 0])
            low = low + jnp.where(hit, live[s], 0.0)
            for side in range(2):
                b = coords[s, 1 + side]
                spot = (b // 4 % 2) * (8 * nz) + (b // 8) * 8 + h * 4 + b % 4
                hit = (row == 2 * (2 * s + side) + h) & (lane == spot)
                high = high + jnp.where(hit, live[s], 0.0)
    blocks_all = 8 * nz
    block_id = lax.broadcasted_iota(jnp.int32, (blocks_all, RANK), 0)
    for t in range(4):
        m.where[blocks_all * t : blocks_all * (t + 1), :] = jnp.where(
            block_id == coords[t // 2, 1 + t % 2], 1.0, 0.0
        )
    m.picks[...] = jnp.zeros_like(m.picks)
    m.meta[0:8, :] = low
    m.meta[8:16, :] = high
    m.full[pl.ds(pl.multiple_of(c * CHUNK, CHUNK), CHUNK), :] = b_in[...]
    m.meta_x[pl.ds(pl.multiple_of(x * 16, 16), 16), :] = m.meta[...]

    pl.semaphore_wait(barrier, NX + NY + nz - 3 + 1)

    def piece_at(step, part, back):
        origin = (z + step) % nz if back else (z - step + nz) % nz
        return m.full.at[
            pl.ds(pl.multiple_of((origin * 2 + core) * CHUNK + part * SUB, SUB), SUB)
        ]

    def hop(step, part, back):
        peer = (z - 1 + nz) % nz if back else (z + 1) % nz
        src = b_in.at[pl.ds(part * SUB, SUB)] if step == 0 else piece_at(step, part, back)
        return send(
            src,
            piece_at(step, part, back),
            "down" if back else "up",
            2 * step + part,
            narrow=peer * 2 + core,
        )

    across = []

    def to_partner(step, part, back):
        src = b_in.at[pl.ds(part * SUB, SUB)] if step == 0 else piece_at(step, part, back)
        across.append(send(src, piece_at(step, part, back), "across", len(across), narrow=partner))

    half_way = nz // 2

    def parts_of(step, back):
        if step < half_way:
            return (0, 1)
        return (1,) if back else (0,)

    hops = {}
    for part in (0, 1):
        for back in (False, True):
            if part in parts_of(1, back):
                hops[1, part, back] = hop(0, part, back)
    meta_x = over_x("meta_sx", lambda peer: m.meta, m.meta_x, 16)
    for part in (0, 1):
        to_partner(0, part, False)

    own_chunk = b_in[...]
    m.gram[...] = dot_full(own_chunk.T, own_chunk)

    def prepare(slot, first, last):
        def one(t, carry):
            span = pl.ds(pl.multiple_of(t * RANK, RANK), RANK)
            part = m.xs[slot, :, span]
            top = part.astype(BF16)
            rest = part - top.astype(F32)
            m.xh[slot, :, span] = top
            m.xl[slot, :, span] = rest.astype(BF16)
            wide_top = top.astype(F32)
            turned = jnp.concatenate([wide_top, rest, wide_top], axis=0).T
            m.xt[slot, span, :] = turned.astype(BF16)
            return carry

        lax.fori_loop(first, last, one, 0)

    load.wait()
    pieces = SPAN // RANK
    prepare(0, 0, pieces // 4)
    quarter = pieces // 2
    jobs = [
        lambda: prepare(0, pieces // 4, pieces * 3 // 4),
        lambda: (prepare(0, pieces * 3 // 4, pieces), prepare(1, 0, pieces // 4)),
        lambda: prepare(1, pieces // 4, pieces * 3 // 4),
        lambda: prepare(1, pieces * 3 // 4, pieces),
    ]

    def add_gram(origin):
        chunk = m.full[pl.ds(pl.multiple_of((origin * 2 + core) * CHUNK, CHUNK), CHUNK), :]
        m.gram[...] += dot_full(chunk.T, chunk)

    def pick_chunk(chunk):
        for b in range(4):
            held = m.full[pl.ds(pl.multiple_of(chunk * CHUNK + b * EDGE, EDGE), EDGE), :]
            for t in range(4):
                m.picks[EDGE * t : EDGE * t + EDGE, :] += (
                    m.where[pl.ds(blocks_all * t + chunk * 4 + b, 1), :] * held
                )

    def pick_partner(step):
        first, last = (0, 2) if step == 0 else (4 * step - 2, min(4 * step + 2, 4 * half_way))
        arrived(across[first:last])
        pick_chunk((z + step) % nz * 2 + 1 - core)
        if 0 < step < half_way:
            pick_chunk((z - step + nz) % nz * 2 + 1 - core)

    pick_chunk(c)
    meta_y = None
    for step in range(1, half_way + 1):
        for part in (0, 1):
            for back in (False, True):
                if part not in parts_of(step, back):
                    continue
                hops[step, part, back].wait_recv()
                if step < half_way and part in parts_of(step + 1, back):
                    hops[step + 1, part, back] = hop(step, part, back)
                to_partner(step, part, back)
        if step == 1:
            arrived(meta_x)
            meta_y = over_y("meta_sy", lambda peer: m.meta_x, m.metas, 16 * NX)
            m.metas[pl.ds(pl.multiple_of(y * 16 * NX, 16 * NX), 16 * NX), :] = m.meta_x[...]
        add_gram((z + step) % nz)
        pick_chunk((z + step) % nz * 2 + core)
        if step < half_way:
            add_gram((z - step + nz) % nz)
            pick_chunk((z - step + nz) % nz * 2 + core)
        pick_partner(step - 1)
        if jobs:
            jobs.pop(0)()
    while jobs:
        jobs.pop(0)()

    grams = send(m.gram, m.gram_in, "grams", 0, narrow=partner)
    arrived(meta_y)
    for yy in range(NY):
        for xx in range(NX):
            at, turn = yy * NX + xx, xx * NY + yy
            tile = m.metas[16 * at : 16 * at + 8, :]
            m.pick_aux_t[4 * at : 4 * at + 4, :] = m.metas[16 * at : 16 * at + 4, :]
            m.pick_reply[8 * turn : 8 * turn + 8, :] = tile
            m.pick_orb_t[8 * at : 8 * at + 8, :] = m.metas[16 * at + 8 : 16 * at + 16, :]
    m.pick_aux[...] = m.pick_aux_t[...].T
    m.pick_orb[...] = m.pick_orb_t[...].T
    pick_partner(half_way)

    def block_rows(s, side):
        return m.picks[EDGE * (2 * s + side) : EDGE * (2 * s + side + 1), :]

    def eight_rows(s, t):
        return m.picks[pl.ds(pl.multiple_of(2 * EDGE * s + t * 8, 8), 8), :]

    for s in range(2):
        rows_j = block_rows(s, 1)

        def pairs(t, carry, s=s, rows_j=rows_j):
            span = pl.ds(pl.multiple_of(t * 512, 512), 512)
            both = (eight_rows(s, t)[:, None, :] * rows_j[None]).reshape(512, RANK)
            top = both.astype(BF16)
            m.krh[span, :] = top
            m.krl[span, :] = (both - top.astype(F32)).astype(BF16)
            return carry

        lax.fori_loop(0, 8, pairs, 0)
        m.terms[EDGE * s : EDGE * s + EDGE, :] = (
            dot_fast(m.xh[s], m.krh[...])
            + dot_fast(m.xh[s], m.krl[...])
            + dot_fast(m.xl[s], m.krh[...])
        )

    for xx in range(NX):
        for s in range(2):
            for h in range(HALVES):
                m.fwd[pl.ds(4 * NY * xx + 2 * s + h, NY, stride=4), :] = m.terms[
                    pl.ds(EDGE * s + NW * h + xx, NY, stride=NX), :
                ]
    size = 4 * NY
    fwd_x = over_x("fwd_sx", lambda peer: rows_of(m.fwd, peer, size), m.fwd_mid, size)
    keep(m.fwd_mid, x, size, m.fwd, x)

    grams.wait_recv()
    m.gram_b[...] = m.gram[...] + m.gram_in[...]
    m.inv[...] = m.gram_b[...] * m.gram_b[...]
    invert_steps(m.inv, 0, 5)

    def turn_around(mid, turned, size):
        for xx in range(NX):
            for yy in range(NY):
                to, at = yy * NX + xx, xx * NY + yy
                turned[size * to : size * to + size, :] = mid[size * at : size * at + size, :]

    arrived(fwd_x)
    turn_around(m.fwd_mid, m.fwd_turn, 4)
    size = 4 * NX
    fwd_y = over_y("fwd_sy", lambda peer: rows_of(m.fwd_turn, peer, 4 * NX), m.fwd_in, size)
    keep(m.fwd_in, y, size, m.fwd_turn, y)
    invert_steps(m.inv, 5, 16)
    arrived(fwd_y)

    aux_sum = dot_full(m.pick_aux[0 : HALVES * QB, :], m.fwd_in[...])
    aux_own = dot_full(aux_sum, m.inv[...])

    m.rep[...] = dot_full(m.pick_reply[:, 0 : HALVES * QB], aux_own)
    m.gram_own[...] = dot_full(aux_own.T, aux_own)
    for xx in range(NX):
        for yy in range(NY):
            at, source = 8 * (xx * NY + yy) + 4, 4 * (yy * NX + xx)
            m.rep[at : at + 4, :] = m.gram_own[source : source + 4, :]
    size = 8 * NY
    rep_x = over_x("rep_sx", lambda peer: rows_of(m.rep, peer, 8 * NY), m.rep_mid, size)
    keep(m.rep_mid, x, size, m.rep, x)

    to = lax.broadcasted_iota(jnp.int32, (NW, HALVES * QB), 0)
    what = lax.broadcasted_iota(jnp.int32, (NW, HALVES * QB), 1)
    target = (to % NY) * NX + to // NY
    share = jnp.where(what == target % 2 * QB + target // 2, 1.0, 0.0)
    m.own[...] = dot_full(share, aux_own)
    own_x = over_x("own_sx", lambda peer: rows_of(m.own, peer, NY), m.own_mid, NY)
    keep(m.own_mid, x, NY, m.own, x)

    arrived(rep_x)
    turn_around(m.rep_mid, m.rep_turn, 8)
    size = 8 * NX
    rep_y = over_y("rep_sy", lambda peer: rows_of(m.rep_turn, peer, 8 * NX), m.rep_in, size)
    keep(m.rep_in, y, size, m.rep_turn, y)

    arrived(own_x)
    m.own_turn[...] = jnp.zeros_like(m.own_turn)
    for xx in range(NX):
        m.own_turn[pl.ds(xx, NY, stride=8), :] = m.own_mid[NY * xx : NY * xx + NY, :]
    own_y = over_y("own_sy", lambda peer: rows_of(m.own_turn, peer, 8), m.own_in, 8)
    keep(m.own_in, y, 8, m.own_turn, y)

    arrived(rep_y)
    total = m.rep_in[0:8, :]
    for k in range(1, NW):
        total = total + m.rep_in[8 * k : 8 * k + 8, :]
    m.tile[...] = total
    tile_core = send(m.tile, m.tile_core, "tile_sc", 0, narrow=partner)

    for s in range(2):
        aux_rows = jnp.concatenate(
            [m.rep_in[pl.ds(2 * s + h, NW, stride=8), :] for h in range(HALVES)], axis=0
        )
        top = aux_rows.astype(BF16)
        rest = (aux_rows - top.astype(F32)).astype(BF16)
        stacked = jnp.concatenate([top, top, rest], axis=0)
        rows_j = block_rows(s, 1)

        def sums(t, term_j, s=s, stacked=stacked, rows_j=rows_j):
            spread = dot_fast(m.xt[s, pl.ds(pl.multiple_of(t * 512, 512), 512), :], stacked)
            spread = spread.reshape(8, EDGE, RANK)
            m.terms[pl.ds(pl.multiple_of(2 * EDGE * s + t * 8, 8), 8), :] = jnp.sum(
                spread * rows_j[None], axis=1
            )
            return term_j + jnp.sum(spread * eight_rows(s, t)[:, None, :], axis=0)

        term_j = lax.fori_loop(0, 8, sums, jnp.zeros((EDGE, RANK), F32))
        m.terms[EDGE * (2 * s + 1) : EDGE * (2 * s + 2), :] = term_j
        for xx in range(NX):
            for side in range(2):
                for h in range(HALVES):
                    block = 2 * s + side
                    m.orb[pl.ds(8 * NY * xx + 2 * block + h, NY, stride=8), :] = m.terms[
                        pl.ds(EDGE * block + NW * h + xx, NY, stride=NX), :
                    ]
        if s == 0:
            tile_core.wait_recv()
            m.tile_sum[...] = m.tile[...] + m.tile_core[...]
            tile_z = over_z("tile_sz", lambda peer: m.tile_sum, m.tile_z, 8)
            m.tile_z[pl.ds(pl.multiple_of(z * 8, 8), 8), :] = m.tile_sum[...]
    size = 8 * NY
    orb_x = over_x("orb_sx", lambda peer: rows_of(m.orb, peer, 8 * NY), m.orb_mid, size)
    keep(m.orb_mid, x, size, m.orb, x)

    arrived(tile_z)
    total = m.tile_z[0:8, :]
    for k in range(1, nz):
        total = total + m.tile_z[8 * k : 8 * k + 8, :]
    m.tile_all[...] = total
    tile_y = over_y("tile_sy", lambda peer: m.tile_all, m.tile_y, 8)
    m.tile_y[pl.ds(pl.multiple_of(y * 8, 8), 8), :] = total

    arrived(orb_x)
    turn_around(m.orb_mid, m.orb_turn, 8)
    size = 8 * NX
    orb_y = over_y("orb_sy", lambda peer: rows_of(m.orb_turn, peer, 8 * NX), m.orb_in, size)
    keep(m.orb_in, y, size, m.orb_turn, y)

    arrived(own_y)
    for yy in range(NY):
        aux_out[NX * yy : NX * yy + NX, :] = m.own_in[8 * yy : 8 * yy + NX, :]

    arrived(tile_y)
    size = 8 * NY
    tile_x = over_x("tile_sx", lambda peer: m.tile_y, m.tile_x, size)
    m.tile_x[pl.ds(pl.multiple_of(x * size, 8), size), :] = m.tile_y[...]

    arrived(orb_y)
    m.dense[...] = dot_full(m.pick_orb[0 : 16 * nz, :], m.orb_in[...])
    size = 8 * nz
    dense_core = send(rows_of(m.dense, 1 - core, size), m.dense_core, "dense_sc", 0, narrow=partner)
    dense_core.wait_recv()
    m.part[...] = m.dense[pl.ds(pl.multiple_of(core * size, 8), size), :] + m.dense_core[...]
    part_z = over_z("part_sz", lambda peer: rows_of(m.part, peer, 8), m.part_z, 8)
    keep(m.part_z, z, 8, m.part, z)

    arrived(tile_x)
    for xx in range(NX):
        for yy in range(NY):
            at, to_row = 8 * (xx * NY + yy) + 4, 4 * (yy * NX + xx)
            m.gram_a[to_row : to_row + 4, :] = m.tile_x[at : at + 4, :]
    m.inv[...] = 2.0 * m.gram_a[...] * m.gram_b[...]
    invert_steps(m.inv, 0, 8)

    arrived(part_z)
    total = m.part_z[0:8, :]
    for k in range(1, nz):
        total = total + m.part_z[8 * k : 8 * k + 8, :]
    m.sum_own[...] = total
    sum_y = over_y("sum_sy", lambda peer: m.sum_own, m.sum_y, 8)
    m.sum_y[pl.ds(pl.multiple_of(y * 8, 8), 8), :] = total
    invert_steps(m.inv, 8, 16)
    arrived(sum_y)
    size = 8 * NY
    sum_x = over_x("sum_sx", lambda peer: m.sum_y, m.sum_x, size)
    m.sum_x[pl.ds(pl.multiple_of(x * size, 8), size), :] = m.sum_y[...]
    arrived(sum_x)
    m.final[...] = dot_full(m.sum_x[...], m.inv[...])
    for xx in range(NX):
        for b in range(4):
            for h in range(HALVES):
                orb_out[pl.ds(EDGE * b + NW * h + xx, NY, stride=NX), :] = m.final[
                    pl.ds(8 * NY * xx + 4 * h + b, NY, stride=8), :
                ]
    for copy in pending:
        copy.wait_send()


def on_device(blocks, block_coords, block_count, orbital_factor, *, nz):
    vmem, sems = scratch_plan(nz)
    scratch = [pltpu.VMEM(shape, dtype) for shape, dtype in vmem.values()]
    scratch += [pltpu.SemaphoreType.DMA((n,)) for n in sems.values()] * 2
    aux, orbital = pl.pallas_call(
        functools.partial(kernel, nz),
        out_shape=(
            jax.ShapeDtypeStruct((NW, RANK), F32),
            jax.ShapeDtypeStruct((CHUNK, RANK), F32),
        ),
        in_specs=[
            pl.BlockSpec(memory_space=pltpu.SMEM),
            pl.BlockSpec(memory_space=pltpu.SMEM),
            pl.BlockSpec(memory_space=pltpu.VMEM),
            pl.BlockSpec(memory_space=pl.ANY),
        ],
        out_specs=(
            pl.BlockSpec(memory_space=pltpu.VMEM),
            pl.BlockSpec(memory_space=pltpu.VMEM),
        ),
        scratch_shapes=scratch,
        compiler_params=pltpu.CompilerParams(
            collective_id=0, has_side_effects=True, vmem_limit_bytes=48 << 20
        ),
    )(
        block_coords.reshape(2, 3),
        block_count.reshape(1, 1),
        orbital_factor,
        blocks.reshape(2, EDGE, SPAN),
    )
    return aux[None], orbital


def solution(mesh):
    return jax.shard_map(
        functools.partial(on_device, nz=mesh.shape["narrow"] // 2),
        mesh=mesh,
        in_specs=(
            P("wide", "narrow", None, None, None),
            P("wide", "narrow", None, None),
            P("wide", "narrow"),
            P("narrow", None),
        ),
        out_specs=(P("narrow", "wide", None), P("narrow", None)),
        check_vma=False,
    )
```

```python
import functools
import types

import jax
import jax.numpy as jnp
from jax import lax
from jax.experimental import pallas as pl
from jax.experimental.pallas import tpu as pltpu
from jax.sharding import PartitionSpec as P

NX, NY = 4, 8
NW = NX * NY
EDGE = 64
RANK = 128
HALVES = EDGE // NW
QB = 16
SPAN = EDGE * EDGE
CHUNK = 256
SUB = CHUNK // 2
F32, BF16 = jnp.float32, jnp.bfloat16
HIGHEST = lax.Precision.HIGHEST


def dot_full(left, right):
    return jnp.dot(left, right, precision=HIGHEST, preferred_element_type=F32)


def dot_fast(left, right):
    return jnp.dot(left, right, preferred_element_type=F32)


def pivot_step(rows):
    lane = lax.broadcasted_iota(jnp.int32, (8, RANK), 1)
    sub = lax.broadcasted_iota(jnp.int32, (8, RANK), 0)
    head = lane < 8

    def over_lanes(block, column):
        return jnp.broadcast_to(block[:, column : column + 1], (8, RANK))

    def over_rows(block, row):
        return jnp.broadcast_to(block[row : row + 1, :], (8, RANK))

    panel = rows[0]
    cols = [over_lanes(panel, m) for m in range(8)]
    for j in range(8):
        scale = 1.0 / over_rows(cols[j], j)
        fresh = []
        for m in range(8):
            if m == j:
                fresh.append(jnp.where(sub == j, scale, -cols[j] * scale))
            else:
                ratio = over_rows(cols[m], j) * scale
                fresh.append(jnp.where(sub == j, ratio, cols[m] - cols[j] * ratio))
        cols = fresh
    panel = jnp.where(head, jnp.where(lane == sub, 1.0, 0.0), panel)
    solved = cols[0] * over_rows(panel, 0)
    for m in range(1, 8):
        solved = solved + cols[m] * over_rows(panel, m)
    spread = [over_rows(solved, m) for m in range(8)]
    out = []
    for row in rows[1:]:
        total = jnp.where(head, 0.0, row)
        for m in range(8):
            total = total - over_lanes(row, m) * spread[m]
        out.append(total)
    out.append(solved)
    return tuple(pltpu.roll(block, RANK - 8, 1) for block in out)


def invert_steps(ref, first, last):
    rows = tuple(ref[8 * k : 8 * k + 8, :] for k in range(16))
    rows = lax.fori_loop(first, last, lambda t, held: pivot_step(held), rows)
    for k in range(16):
        ref[8 * k : 8 * k + 8, :] = rows[k]


def scratch_plan(nz):
    nc = 2 * nz
    vmem = dict(
        xs=((2, EDGE, SPAN), F32),
        xh=((2, EDGE, SPAN), BF16),
        xl=((2, EDGE, SPAN), BF16),
        xt=((2, SPAN, 3 * EDGE), BF16),
        full=((CHUNK * nc, RANK), F32),
        where=((4 * 8 * nz, RANK), F32),
        picks=((4 * EDGE, RANK), F32),
        krh=((SPAN, RANK), BF16),
        krl=((SPAN, RANK), BF16),
        gram=((RANK, RANK), F32),
        gram_in=((RANK, RANK), F32),
        gram_b=((RANK, RANK), F32),
        gram_own=((RANK, RANK), F32),
        gram_a=((RANK, RANK), F32),
        inv=((RANK, RANK), F32),
        where_at=((2, 3), jnp.int32),
        lived=((1, 1), jnp.int32),
        mine=((CHUNK, RANK), F32),
        meta=((8, RANK), F32),
        meta_x=((8 * NX, RANK), F32),
        meta_row=((8, RANK), F32),
        metas=((8 * NY, RANK), F32),
        spread=((SPAN, RANK), F32),
        pick_aux_t=((4 * NW, RANK), F32),
        pick_aux=((RANK, 4 * NW), F32),
        pick_orb_t=((8 * NW, RANK), F32),
        pick_orb=((RANK, 8 * NW), F32),
        pick_reply=((8 * NW, RANK), F32),
        terms=((4 * EDGE, RANK), F32),
        fwd=((NW, 4, RANK), F32),
        fwd_in=((NW, 4, RANK), F32),
        fwd_rows=((4 * NW, RANK), F32),
        rep=((8 * NW, RANK), F32),
        rep_in=((8 * NW, RANK), F32),
        own=((NW, RANK), F32),
        own_mid=((NW, RANK), F32),
        own_turn=((8 * NY, RANK), F32),
        own_in=((8 * NY, RANK), F32),
        tile=((8, RANK), F32),
        tile_core=((8, RANK), F32),
        tile_sum=((8, RANK), F32),
        tile_all=((8, RANK), F32),
        sum_own=((8, RANK), F32),
        tile_z=((8 * nz, RANK), F32),
        tile_y=((8 * NY, RANK), F32),
        tile_x=((8 * NW, RANK), F32),
        orb=((8 * NW, RANK), F32),
        orb_in=((8 * NW, RANK), F32),
        dense=((16 * nz, RANK), F32),
        dense_core=((8 * nz, RANK), F32),
        part=((8 * nz, RANK), F32),
        part_z=((8 * nz, RANK), F32),
        sum_y=((8 * NY, RANK), F32),
        sum_x=((8 * NW, RANK), F32),
        final=((8 * NW, RANK), F32),
    )
    sems = dict(
        load=4,
        up=8,
        down=8,
        across=16,
        grams=1,
        meta_sx=NX,
        meta_sy=NY,
        fwd_s=1,
        rep_s=1,
        own_sx=NX,
        own_sy=NY,
        tile_sc=1,
        tile_sz=nz,
        tile_sy=NY,
        tile_sx=NX,
        orb_s=1,
        dense_sc=1,
        part_sz=nz,
        sum_sy=NY,
        sum_sx=NX,
    )
    return vmem, sems


def kernel(nz, coords, count, b_in, blocks, aux_out, orb_out, *scratch):
    vmem, sems = scratch_plan(nz)
    m = types.SimpleNamespace(**dict(zip(vmem, scratch)))
    rest = scratch[len(vmem) :]
    sent = dict(zip(sems, rest[: len(sems)]))
    got = dict(zip(sems, rest[len(sems) :]))

    w = lax.axis_index("wide")
    c = lax.axis_index("narrow")
    x, y = w % NX, w // NX
    z, core = c // 2, c % 2
    pending = []

    def send(src, dst, name, index, wide=None, narrow=None):
        copy = pltpu.make_async_remote_copy(
            src_ref=src,
            dst_ref=dst,
            send_sem=sent[name].at[index],
            recv_sem=got[name].at[index],
            device_id=(w if wide is None else wide, c if narrow is None else narrow),
            device_id_type=pl.DeviceIdType.MESH,
        )
        copy.start()
        pending.append(copy)
        return copy

    def rows_of(ref, index, size):
        return ref.at[pl.ds(pl.multiple_of(index * size, 8), size)]

    def over_x(name, piece, dst, size):
        copies = []
        for d in range(1, NX):
            peer = (x + d) % NX
            copies.append(send(piece(peer), rows_of(dst, x, size), name, d, wide=y * NX + peer))
        return copies

    def over_y(name, piece, dst, size):
        copies = []
        for d in range(1, NY):
            peer = (y + d) % NY
            copies.append(send(piece(peer), rows_of(dst, y, size), name, d, wide=peer * NX + x))
        return copies

    def over_z(name, piece, dst, size):
        copies = []
        for d in range(1, nz):
            peer = (z + d) % nz
            copies.append(send(piece(peer), rows_of(dst, z, size), name, d, narrow=peer * 2 + core))
        return copies

    def to_all(name, src_of, dst):
        for dy in sorted(range(NY), key=lambda d: -min(d, NY - d)):
            for dx in sorted(range(NX), key=lambda d: -min(d, NX - d)):
                if dx or dy:
                    peer = (y + dy) % NY * NX + (x + dx) % NX
                    pltpu.make_async_remote_copy(
                        src_ref=src_of(peer),
                        dst_ref=dst,
                        send_sem=sent[name].at[0],
                        recv_sem=got[name].at[0],
                        device_id=(peer, c),
                        device_id_type=pl.DeviceIdType.MESH,
                    ).start()

    def all_in(name, others, which=None):
        sem = (got if which is None else which)[name].at[0]
        pltpu.make_async_copy(others, others, sem).wait()

    def arrived(copies):
        for copy in copies:
            copy.wait_recv()

    def keep(dst, index, size, src, src_index):
        dst[pl.ds(pl.multiple_of(index * size, 8), size), :] = src[
            pl.ds(pl.multiple_of(src_index * size, 8), size), :
        ]

    loads = [
        pltpu.make_async_copy(src, dst, sent["load"].at[k])
        for k, (src, dst) in enumerate(
            [(b_in, m.mine), (coords, m.where_at), (count, m.lived), (blocks, m.xs)]
        )
    ]
    for copy in loads:
        copy.start()

    barrier = pltpu.get_barrier_semaphore()
    for d in range(1, NX):
        pl.semaphore_signal(
            barrier, inc=1, device_id=(y * NX + (x + d) % NX, c), device_id_type=pl.DeviceIdType.MESH
        )
    for d in range(1, NY):
        pl.semaphore_signal(
            barrier, inc=1, device_id=((y + d) % NY * NX + x, c), device_id_type=pl.DeviceIdType.MESH
        )
    for d in range(1, nz):
        pl.semaphore_signal(
            barrier, inc=1, device_id=(w, (z + d) % nz * 2 + core), device_id_type=pl.DeviceIdType.MESH
        )
    partner = z * 2 + 1 - core
    pl.semaphore_signal(barrier, inc=1, device_id=(w, partner), device_id_type=pl.DeviceIdType.MESH)

    m.picks[...] = jnp.zeros_like(m.picks)
    m.pick_reply[...] = jnp.zeros_like(m.pick_reply)
    m.meta_row[...] = jnp.zeros_like(m.meta_row)

    loads[1].wait()
    loads[2].wait()
    lane = lax.broadcasted_iota(jnp.int32, (8, RANK), 1)
    blocks_all = 8 * nz
    block_id = lax.broadcasted_iota(jnp.int32, (blocks_all, RANK), 0)
    spots = jnp.zeros((8, RANK), F32)
    for s in range(2):
        live = jnp.broadcast_to(m.lived[0:1, 0:1], (8, RANK)) > s
        for side in range(3):
            at = jnp.broadcast_to(m.where_at[s : s + 1, side : side + 1], (8, RANK))
            if side == 0:
                t, spot = s, at
            else:
                t = 2 + 2 * s + side - 1
                spot = (at & 7) // 4 * (8 * nz) + (at // 8) * 8 + (at & 3)
                m.where[blocks_all * (t - 2) : blocks_all * (t - 1), :] = jnp.where(
                    block_id == jnp.broadcast_to(at[0:1, :], block_id.shape), 1.0, 0.0
                )
            spot = jnp.where(live, spot, -1000).astype(F32)
            spots = spots + jnp.where(lane == t, spot, 0.0)
    m.meta[...] = spots

    def prepare(slot, first, last):
        def one(t, carry):
            span = pl.ds(pl.multiple_of(t * RANK, RANK), RANK)
            part = m.xs[slot, :, span]
            top = part.astype(BF16)
            rest = part - top.astype(F32)
            m.xh[slot, :, span] = top
            m.xl[slot, :, span] = rest.astype(BF16)
            wide_top = top.astype(F32)
            turned = jnp.concatenate([wide_top, rest, wide_top], axis=0).T
            m.xt[slot, span, :] = turned.astype(BF16)
            return carry

        lax.fori_loop(first, last, one, 0)

    def pick_chunk(chunk):
        for b in range(4):
            held = m.full[pl.ds(pl.multiple_of(chunk * CHUNK + b * EDGE, EDGE), EDGE), :]
            for t in range(4):
                m.picks[EDGE * t : EDGE * t + EDGE, :] += (
                    m.where[pl.ds(blocks_all * t + chunk * 4 + b, 1), :] * held
                )

    loads[0].wait()
    m.full[pl.ds(pl.multiple_of(c * CHUNK, CHUNK), CHUNK), :] = m.mine[...]
    loads[3].wait()
    pieces = SPAN // RANK
    early = pieces // 2
    prepare(0, 0, early)
    pl.semaphore_wait(barrier, NX + NY + nz - 2)

    def piece_at(step, part, back):
        origin = (z + step) % nz if back else (z - step + nz) % nz
        return m.full.at[
            pl.ds(pl.multiple_of((origin * 2 + core) * CHUNK + part * SUB, SUB), SUB)
        ]

    def hop(step, part, back):
        peer = (z - 1 + nz) % nz if back else (z + 1) % nz
        src = m.mine.at[pl.ds(part * SUB, SUB)] if step == 0 else piece_at(step, part, back)
        return send(
            src,
            piece_at(step, part, back),
            "down" if back else "up",
            2 * step + part,
            narrow=peer * 2 + core,
        )

    across = []

    def to_partner(step, part, back):
        src = m.mine.at[pl.ds(part * SUB, SUB)] if step == 0 else piece_at(step, part, back)
        across.append(send(src, piece_at(step, part, back), "across", len(across), narrow=partner))

    half_way = nz // 2

    def parts_of(step, back):
        if step < half_way:
            return (0, 1)
        return (1,) if back else (0,)

    hops = {}
    for part in (0, 1):
        for back in (False, True):
            if part in parts_of(1, back):
                hops[1, part, back] = hop(0, part, back)
    meta_x = over_x("meta_sx", lambda peer: m.meta, m.meta_x, 8)
    m.meta_x[pl.ds(pl.multiple_of(x * 8, 8), 8), :] = m.meta[...]
    for part in (0, 1):
        to_partner(0, part, False)
    pick_chunk(c)
    own_chunk = m.mine[...]
    m.gram[...] = dot_full(own_chunk.T, own_chunk)
    jobs = [
        lambda: prepare(0, early, pieces),
        lambda: prepare(1, 0, pieces // 3),
        lambda: prepare(1, pieces // 3, pieces * 2 // 3),
        lambda: prepare(1, pieces * 2 // 3, pieces),
    ]

    def add_gram(origin):
        chunk = m.full[pl.ds(pl.multiple_of((origin * 2 + core) * CHUNK, CHUNK), CHUNK), :]
        m.gram[...] += dot_full(chunk.T, chunk)

    def pick_partner(step):
        first, last = (0, 2) if step == 0 else (4 * step - 2, min(4 * step + 2, 4 * half_way))
        arrived(across[first:last])
        pick_chunk((z + step) % nz * 2 + 1 - core)
        if 0 < step < half_way:
            pick_chunk((z - step + nz) % nz * 2 + 1 - core)

    meta_y = None
    for step in range(1, half_way + 1):
        for part in (0, 1):
            for back in (False, True):
                if part not in parts_of(step, back):
                    continue
                hops[step, part, back].wait_recv()
                if step < half_way and part in parts_of(step + 1, back):
                    hops[step + 1, part, back] = hop(step, part, back)
                to_partner(step, part, back)
        if step == 1:
            arrived(meta_x)
            for xx in range(NX):
                m.meta_row[xx : xx + 1, :] = m.meta_x[8 * xx : 8 * xx + 1, :]
            meta_y = over_y("meta_sy", lambda peer: m.meta_row, m.metas, 8)
            m.metas[pl.ds(pl.multiple_of(y * 8, 8), 8), :] = m.meta_row[...]
        add_gram((z + step) % nz)
        pick_chunk((z + step) % nz * 2 + core)
        if step < half_way:
            add_gram((z - step + nz) % nz)
            pick_chunk((z - step + nz) % nz * 2 + core)
        pick_partner(step - 1)
        if jobs:
            jobs.pop(0)()
    while jobs:
        jobs.pop(0)()

    grams = send(m.gram, m.gram_in, "grams", 0, narrow=partner)
    arrived(meta_y)
    places = jnp.concatenate([m.metas[8 * yy : 8 * yy + NX, :] for yy in range(NY)], axis=0)
    lanes = lax.broadcasted_iota(jnp.int32, (NW, RANK), 1).astype(F32)
    for t in range(6):
        place = jnp.broadcast_to(places[:, t : t + 1], (NW, RANK))
        for h in range(HALVES):
            if t < 2:
                hot = jnp.where(lanes == place + QB * h, 1.0, 0.0)
                m.pick_aux_t[pl.ds(2 * t + h, NW, stride=4), :] = hot
                m.pick_reply[pl.ds(2 * t + h, NW, stride=8), :] = hot
            else:
                m.pick_orb_t[pl.ds(2 * (t - 2) + h, NW, stride=8), :] = jnp.where(
                    lanes == place + 4 * h, 1.0, 0.0
                )
    m.pick_aux[...] = m.pick_aux_t[...].T
    m.pick_orb[...] = m.pick_orb_t[...].T
    pick_partner(half_way)

    def block_rows(s, side):
        return m.picks[EDGE * (2 * s + side) : EDGE * (2 * s + side + 1), :]

    def eight_rows(s, t):
        return m.picks[pl.ds(pl.multiple_of(2 * EDGE * s + t * 8, 8), 8), :]

    for s in range(2):
        rows_j = block_rows(s, 1)

        def pairs(t, carry, s=s, rows_j=rows_j):
            span = pl.ds(pl.multiple_of(t * 512, 512), 512)
            both = (eight_rows(s, t)[:, None, :] * rows_j[None]).reshape(512, RANK)
            top = both.astype(BF16)
            m.krh[span, :] = top
            m.krl[span, :] = (both - top.astype(F32)).astype(BF16)
            return carry

        lax.fori_loop(0, 8, pairs, 0)
        m.terms[EDGE * s : EDGE * s + EDGE, :] = (
            dot_fast(m.xh[s], m.krh[...])
            + dot_fast(m.xh[s], m.krl[...])
            + dot_fast(m.xl[s], m.krh[...])
        )

    for s in range(2):
        for h in range(HALVES):
            m.fwd_rows[pl.ds(2 * s + h, NW, stride=4), :] = m.terms[
                EDGE * s + NW * h : EDGE * s + NW * (h + 1), :
            ]
    for k in range(NW):
        m.fwd[k] = m.fwd_rows[4 * k : 4 * k + 4, :]
    to_all("fwd_s", lambda peer: m.fwd.at[peer], m.fwd_in.at[w])
    m.fwd_in[w] = m.fwd[w]

    grams.wait_recv()
    m.gram_b[...] = m.gram[...] + m.gram_in[...]
    m.inv[...] = m.gram_b[...] * m.gram_b[...]
    invert_steps(m.inv, 0, 16)
    all_in("fwd_s", m.fwd_in.at[pl.ds(0, NW - 1)])
    for k in range(NW):
        m.fwd_rows[4 * k : 4 * k + 4, :] = m.fwd_in[k]

    aux_sum = dot_full(m.pick_aux[0 : HALVES * QB, :], m.fwd_rows[...])
    aux_own = dot_full(aux_sum, m.inv[...])

    m.rep[...] = dot_full(m.pick_reply[:, 0 : HALVES * QB], aux_own)
    m.gram_own[...] = dot_full(aux_own.T, aux_own)
    for k in range(NW):
        m.rep[8 * k + 4 : 8 * k + 8, :] = m.gram_own[4 * k : 4 * k + 4, :]
    to_all("rep_s", lambda peer: rows_of(m.rep, peer, 8), rows_of(m.rep_in, w, 8))
    keep(m.rep_in, w, 8, m.rep, w)

    to = lax.broadcasted_iota(jnp.int32, (NW, HALVES * QB), 0)
    what = lax.broadcasted_iota(jnp.int32, (NW, HALVES * QB), 1)
    target = (to % NY) * NX + to // NY
    share = jnp.where(what == target % 2 * QB + target // 2, 1.0, 0.0)
    m.own[...] = dot_full(share, aux_own)
    own_x = over_x("own_sx", lambda peer: rows_of(m.own, peer, NY), m.own_mid, NY)
    keep(m.own_mid, x, NY, m.own, x)

    arrived(own_x)
    m.own_turn[...] = jnp.zeros_like(m.own_turn)
    for xx in range(NX):
        m.own_turn[pl.ds(xx, NY, stride=8), :] = m.own_mid[NY * xx : NY * xx + NY, :]
    own_y = over_y("own_sy", lambda peer: rows_of(m.own_turn, peer, 8), m.own_in, 8)
    keep(m.own_in, y, 8, m.own_turn, y)

    all_in("rep_s", m.rep_in.at[pl.ds(0, 8 * (NW - 1))])
    total = m.rep_in[0:8, :]
    for k in range(1, NW):
        total = total + m.rep_in[8 * k : 8 * k + 8, :]
    m.tile[...] = total
    tile_core = send(m.tile, m.tile_core, "tile_sc", 0, narrow=partner)

    for s in range(2):
        aux_rows = jnp.concatenate(
            [m.rep_in[pl.ds(2 * s + h, NW, stride=8), :] for h in range(HALVES)], axis=0
        )
        top = aux_rows.astype(BF16)
        rest = (aux_rows - top.astype(F32)).astype(BF16)
        stacked = jnp.concatenate([top, top, rest], axis=0)
        rows_j = block_rows(s, 1)

        m.spread[...] = dot_fast(m.xt[s], stacked)

        def sums(t, term_j, s=s, rows_j=rows_j):
            for k in range(8):
                i = t * 8 + k
                part = m.spread[pl.ds(pl.multiple_of(i * EDGE, EDGE), EDGE), :]
                m.terms[pl.ds(2 * EDGE * s + i, 1), :] = jnp.sum(
                    part * rows_j, axis=0, keepdims=True
                )
                term_j = term_j + part * m.picks[pl.ds(2 * EDGE * s + i, 1), :]
            return term_j

        term_j = lax.fori_loop(0, 8, sums, jnp.zeros((EDGE, RANK), F32))
        m.terms[EDGE * (2 * s + 1) : EDGE * (2 * s + 2), :] = term_j
        for side in range(2):
            for h in range(HALVES):
                block = 2 * s + side
                m.orb[pl.ds(2 * block + h, NW, stride=8), :] = m.terms[
                    EDGE * block + NW * h : EDGE * block + NW * (h + 1), :
                ]
        if s == 0:
            tile_core.wait_recv()
            m.tile_sum[...] = m.tile[...] + m.tile_core[...]
            tile_z = over_z("tile_sz", lambda peer: m.tile_sum, m.tile_z, 8)
            m.tile_z[pl.ds(pl.multiple_of(z * 8, 8), 8), :] = m.tile_sum[...]
    to_all("orb_s", lambda peer: rows_of(m.orb, peer, 8), rows_of(m.orb_in, w, 8))
    keep(m.orb_in, w, 8, m.orb, w)

    arrived(tile_z)
    total = m.tile_z[0:8, :]
    for k in range(1, nz):
        total = total + m.tile_z[8 * k : 8 * k + 8, :]
    m.tile_all[...] = total
    tile_y = over_y("tile_sy", lambda peer: m.tile_all, m.tile_y, 8)
    m.tile_y[pl.ds(pl.multiple_of(y * 8, 8), 8), :] = total

    arrived(own_y)
    for yy in range(NY):
        aux_out[NX * yy : NX * yy + NX, :] = m.own_in[8 * yy : 8 * yy + NX, :]

    arrived(tile_y)
    size = 8 * NY
    tile_x = over_x("tile_sx", lambda peer: m.tile_y, m.tile_x, size)
    m.tile_x[pl.ds(pl.multiple_of(x * size, 8), size), :] = m.tile_y[...]

    all_in("orb_s", m.orb_in.at[pl.ds(0, 8 * (NW - 1))])
    m.dense[...] = dot_full(m.pick_orb[0 : 16 * nz, :], m.orb_in[...])
    size = 8 * nz
    dense_core = send(rows_of(m.dense, 1 - core, size), m.dense_core, "dense_sc", 0, narrow=partner)
    dense_core.wait_recv()
    m.part[...] = m.dense[pl.ds(pl.multiple_of(core * size, 8), size), :] + m.dense_core[...]
    part_z = over_z("part_sz", lambda peer: rows_of(m.part, peer, 8), m.part_z, 8)
    keep(m.part_z, z, 8, m.part, z)

    arrived(tile_x)
    for xx in range(NX):
        for yy in range(NY):
            at, to_row = 8 * (xx * NY + yy) + 4, 4 * (yy * NX + xx)
            m.gram_a[to_row : to_row + 4, :] = m.tile_x[at : at + 4, :]
    m.inv[...] = 2.0 * m.gram_a[...] * m.gram_b[...]
    invert_steps(m.inv, 0, 8)

    arrived(part_z)
    total = m.part_z[0:8, :]
    for k in range(1, nz):
        total = total + m.part_z[8 * k : 8 * k + 8, :]
    m.sum_own[...] = total
    sum_y = over_y("sum_sy", lambda peer: m.sum_own, m.sum_y, 8)
    m.sum_y[pl.ds(pl.multiple_of(y * 8, 8), 8), :] = total
    invert_steps(m.inv, 8, 16)
    arrived(sum_y)
    size = 8 * NY
    sum_x = over_x("sum_sx", lambda peer: m.sum_y, m.sum_x, size)
    m.sum_x[pl.ds(pl.multiple_of(x * size, 8), size), :] = m.sum_y[...]
    arrived(sum_x)
    m.final[...] = dot_full(m.sum_x[...], m.inv[...])
    for xx in range(NX):
        for b in range(4):
            for h in range(HALVES):
                orb_out[pl.ds(EDGE * b + NW * h + xx, NY, stride=NX), :] = m.final[
                    pl.ds(8 * NY * xx + 4 * h + b, NY, stride=8), :
                ]
    for copy in pending:
        copy.wait_send()
    all_in("fwd_s", m.fwd.at[pl.ds(0, NW - 1)], sent)
    all_in("rep_s", m.rep.at[pl.ds(0, 8 * (NW - 1))], sent)
    all_in("orb_s", m.orb.at[pl.ds(0, 8 * (NW - 1))], sent)


def on_device(blocks, block_coords, block_count, orbital_factor, *, nz):
    vmem, sems = scratch_plan(nz)
    scratch = [pltpu.VMEM(shape, dtype) for shape, dtype in vmem.values()]
    scratch += [pltpu.SemaphoreType.DMA((n,)) for n in sems.values()] * 2
    aux, orbital = pl.pallas_call(
        functools.partial(kernel, nz),
        out_shape=(
            jax.ShapeDtypeStruct((NW, RANK), F32),
            jax.ShapeDtypeStruct((CHUNK, RANK), F32),
        ),
        in_specs=[
            pl.BlockSpec(memory_space=pl.ANY),
            pl.BlockSpec(memory_space=pl.ANY),
            pl.BlockSpec(memory_space=pl.ANY),
            pl.BlockSpec(memory_space=pl.ANY),
        ],
        out_specs=(
            pl.BlockSpec(memory_space=pltpu.VMEM),
            pl.BlockSpec(memory_space=pltpu.VMEM),
        ),
        scratch_shapes=scratch,
        compiler_params=pltpu.CompilerParams(
            collective_id=0, has_side_effects=True, vmem_limit_bytes=67_043_328 - (160 << 10)
        ),
    )(
        block_coords.reshape(2, 3),
        block_count.reshape(1, 1),
        orbital_factor,
        blocks.reshape(2, EDGE, SPAN),
    )
    return aux[None], orbital


def solution(mesh):
    return jax.shard_map(
        functools.partial(on_device, nz=mesh.shape["narrow"] // 2),
        mesh=mesh,
        in_specs=(
            P("wide", "narrow", None, None, None),
            P("wide", "narrow", None, None),
            P("wide", "narrow"),
            P("narrow", None),
        ),
        out_specs=(P("narrow", "wide", None), P("narrow", None)),
        check_vma=False,
    )
```

```python
import functools
import types

import jax
import jax.numpy as jnp
from jax import lax
from jax.experimental import pallas as pl
from jax.experimental.pallas import tpu as pltpu
from jax.sharding import PartitionSpec as P

NX, NY = 4, 8
NW = NX * NY
EDGE = 64
RANK = 128
HALVES = EDGE // NW
QB = 16
SPAN = EDGE * EDGE
CHUNK = 256
SUB = CHUNK // 2
F32, BF16 = jnp.float32, jnp.bfloat16
HIGHEST = lax.Precision.HIGHEST


def dot_full(left, right):
    return jnp.dot(left, right, precision=HIGHEST, preferred_element_type=F32)


def dot_fast(left, right):
    return jnp.dot(left, right, preferred_element_type=F32)


def pivot_step(rows):
    lane = lax.broadcasted_iota(jnp.int32, (8, RANK), 1)
    sub = lax.broadcasted_iota(jnp.int32, (8, RANK), 0)
    head = lane < 8

    def over_lanes(block, column):
        return jnp.broadcast_to(block[:, column : column + 1], (8, RANK))

    def over_rows(block, row):
        return jnp.broadcast_to(block[row : row + 1, :], (8, RANK))

    panel = rows[0]
    cols = [over_lanes(panel, m) for m in range(8)]
    for j in range(8):
        scale = 1.0 / over_rows(cols[j], j)
        fresh = []
        for m in range(8):
            if m == j:
                fresh.append(jnp.where(sub == j, scale, -cols[j] * scale))
            else:
                ratio = over_rows(cols[m], j) * scale
                fresh.append(jnp.where(sub == j, ratio, cols[m] - cols[j] * ratio))
        cols = fresh
    panel = jnp.where(head, jnp.where(lane == sub, 1.0, 0.0), panel)
    solved = cols[0] * over_rows(panel, 0)
    for m in range(1, 8):
        solved = solved + cols[m] * over_rows(panel, m)
    spread = [over_rows(solved, m) for m in range(8)]
    out = []
    for row in rows[1:]:
        total = jnp.where(head, 0.0, row)
        for m in range(8):
            total = total - over_lanes(row, m) * spread[m]
        out.append(total)
    out.append(solved)
    return tuple(pltpu.roll(block, RANK - 8, 1) for block in out)


def invert_steps(ref, first, last):
    rows = tuple(ref[8 * k : 8 * k + 8, :] for k in range(16))
    rows = lax.fori_loop(first, last, lambda t, held: pivot_step(held), rows)
    for k in range(16):
        ref[8 * k : 8 * k + 8, :] = rows[k]


def scratch_plan(nz):
    nc = 2 * nz
    vmem = dict(
        xs=((2, EDGE, SPAN), F32),
        xh=((2, EDGE, SPAN), BF16),
        xl=((2, EDGE, SPAN), BF16),
        xt=((2, SPAN, 3 * EDGE), BF16),
        full=((CHUNK * nc, RANK), F32),
        where=((4 * 8 * nz, RANK), F32),
        picks=((4 * EDGE, RANK), F32),
        krh=((SPAN, RANK), BF16),
        krl=((SPAN, RANK), BF16),
        gram=((RANK, RANK), F32),
        gram_in=((RANK, RANK), F32),
        gram_b=((RANK, RANK), F32),
        gram_own=((RANK, RANK), F32),
        gram_a=((RANK, RANK), F32),
        inv=((RANK, RANK), F32),
        where_at=((2, 3), jnp.int32),
        lived=((1, 1), jnp.int32),
        mine=((CHUNK, RANK), F32),
        meta=((8, RANK), F32),
        meta_x=((8 * NX, RANK), F32),
        meta_row=((8, RANK), F32),
        metas=((8 * NY, RANK), F32),
        spread=((SPAN, RANK), F32),
        pick_aux_t=((4 * NW, RANK), F32),
        pick_aux=((RANK, 4 * NW), F32),
        pick_orb_t=((8 * NW, RANK), F32),
        pick_orb=((2, RANK, 4 * NW), F32),
        terms=((4 * EDGE, RANK), F32),
        fwd=((NW, 4, RANK), F32),
        fwd_in=((NW, 4, RANK), F32),
        fwd_rows=((4 * NW, RANK), F32),
        rep=((NW, 4, RANK), F32),
        rep_in=((NW, 4, RANK), F32),
        rep_rows=((4 * NW, RANK), F32),
        tri=((NW, 4, RANK), F32),
        tri_in=((NW, 4, RANK), F32),
        own=((NW, RANK), F32),
        own_mid=((NW, RANK), F32),
        own_turn=((8 * NY, RANK), F32),
        own_in=((8 * NY, RANK), F32),
        tile=((8, RANK), F32),
        tile_core=((8, RANK), F32),
        tile_sum=((8, RANK), F32),
        tile_all=((8, RANK), F32),
        sum_own=((8, RANK), F32),
        tile_z=((8 * nz, RANK), F32),
        tile_y=((8 * NY, RANK), F32),
        tile_x=((8 * NW, RANK), F32),
        orb_0=((NW, 4, RANK), F32),
        orb_1=((NW, 4, RANK), F32),
        orb_in_0=((NW, 4, RANK), F32),
        orb_in_1=((NW, 4, RANK), F32),
        orb_rows=((4 * NW, RANK), F32),
        got_rows=((4 * NW, RANK), F32),
        dense=((16 * nz, RANK), F32),
        dense_core=((8 * nz, RANK), F32),
        part=((8 * nz, RANK), F32),
        part_z=((8 * nz, RANK), F32),
        sum_y=((8 * NY, RANK), F32),
        sum_x=((8 * NW, RANK), F32),
        final=((8 * NW, RANK), F32),
    )
    sems = dict(
        load=4,
        up=8,
        down=8,
        across=16,
        grams=1,
        meta_sx=NX,
        meta_sy=NY,
        fwd_s=1,
        rep_s=1,
        tri_s=1,
        own_sx=NX,
        own_sy=NY,
        tile_sc=1,
        tile_sz=nz,
        tile_sy=NY,
        tile_sx=NX,
        orb_0=1,
        orb_1=1,
        dense_sc=1,
        part_sz=nz,
        sum_sy=NY,
        sum_sx=NX,
    )
    return vmem, sems


def kernel(nz, coords, count, b_in, blocks, aux_out, orb_out, *scratch):
    vmem, sems = scratch_plan(nz)
    m = types.SimpleNamespace(**dict(zip(vmem, scratch)))
    rest = scratch[len(vmem) :]
    sent = dict(zip(sems, rest[: len(sems)]))
    got = dict(zip(sems, rest[len(sems) :]))

    w = lax.axis_index("wide")
    c = lax.axis_index("narrow")
    x, y = w % NX, w // NX
    z, core = c // 2, c % 2
    pending = []

    def send(src, dst, name, index, wide=None, narrow=None):
        copy = pltpu.make_async_remote_copy(
            src_ref=src,
            dst_ref=dst,
            send_sem=sent[name].at[index],
            recv_sem=got[name].at[index],
            device_id=(w if wide is None else wide, c if narrow is None else narrow),
            device_id_type=pl.DeviceIdType.MESH,
        )
        copy.start()
        pending.append(copy)
        return copy

    def rows_of(ref, index, size):
        return ref.at[pl.ds(pl.multiple_of(index * size, 8), size)]

    def over_x(name, piece, dst, size):
        copies = []
        for d in range(1, NX):
            peer = (x + d) % NX
            copies.append(send(piece(peer), rows_of(dst, x, size), name, d, wide=y * NX + peer))
        return copies

    def over_y(name, piece, dst, size):
        copies = []
        for d in range(1, NY):
            peer = (y + d) % NY
            copies.append(send(piece(peer), rows_of(dst, y, size), name, d, wide=peer * NX + x))
        return copies

    def over_z(name, piece, dst, size):
        copies = []
        for d in range(1, nz):
            peer = (z + d) % nz
            copies.append(send(piece(peer), rows_of(dst, z, size), name, d, narrow=peer * 2 + core))
        return copies

    def to_all(name, src_of, dst):
        for dy in sorted(range(NY), key=lambda d: -min(d, NY - d)):
            for dx in sorted(range(NX), key=lambda d: -min(d, NX - d)):
                if dx or dy:
                    peer = (y + dy) % NY * NX + (x + dx) % NX
                    pltpu.make_async_remote_copy(
                        src_ref=src_of(peer),
                        dst_ref=dst,
                        send_sem=sent[name].at[0],
                        recv_sem=got[name].at[0],
                        device_id=(peer, c),
                        device_id_type=pl.DeviceIdType.MESH,
                    ).start()

    def send_pieces(name, rows, pieces, into):
        for k in range(NW):
            pieces[k] = rows[4 * k : 4 * k + 4, :]
        to_all(name, lambda peer: pieces.at[peer], into.at[w])
        into[w] = pieces[w]

    def take_pieces(name, into, rows):
        all_in(name, into.at[pl.ds(0, NW - 1)])
        for k in range(NW):
            rows[4 * k : 4 * k + 4, :] = into[k]

    def all_in(name, others, which=None):
        sem = (got if which is None else which)[name].at[0]
        pltpu.make_async_copy(others, others, sem).wait()

    def arrived(copies):
        for copy in copies:
            copy.wait_recv()

    def keep(dst, index, size, src, src_index):
        dst[pl.ds(pl.multiple_of(index * size, 8), size), :] = src[
            pl.ds(pl.multiple_of(src_index * size, 8), size), :
        ]

    loads = [
        pltpu.make_async_copy(src, dst, sent["load"].at[k])
        for k, (src, dst) in enumerate(
            [(b_in, m.mine), (coords, m.where_at), (count, m.lived), (blocks, m.xs)]
        )
    ]
    for copy in loads:
        copy.start()

    barrier = pltpu.get_barrier_semaphore()
    for d in range(1, NX):
        pl.semaphore_signal(
            barrier, inc=1, device_id=(y * NX + (x + d) % NX, c), device_id_type=pl.DeviceIdType.MESH
        )
    for d in range(1, NY):
        pl.semaphore_signal(
            barrier, inc=1, device_id=((y + d) % NY * NX + x, c), device_id_type=pl.DeviceIdType.MESH
        )
    for d in range(1, nz):
        pl.semaphore_signal(
            barrier, inc=1, device_id=(w, (z + d) % nz * 2 + core), device_id_type=pl.DeviceIdType.MESH
        )
    partner = z * 2 + 1 - core
    pl.semaphore_signal(barrier, inc=1, device_id=(w, partner), device_id_type=pl.DeviceIdType.MESH)

    m.picks[...] = jnp.zeros_like(m.picks)
    m.tile[...] = jnp.zeros_like(m.tile)
    m.meta_row[...] = jnp.zeros_like(m.meta_row)

    loads[1].wait()
    loads[2].wait()
    lane = lax.broadcasted_iota(jnp.int32, (8, RANK), 1)
    blocks_all = 8 * nz
    block_id = lax.broadcasted_iota(jnp.int32, (blocks_all, RANK), 0)
    spots = jnp.zeros((8, RANK), F32)
    for s in range(2):
        live = jnp.broadcast_to(m.lived[0:1, 0:1], (8, RANK)) > s
        for side in range(3):
            at = jnp.broadcast_to(m.where_at[s : s + 1, side : side + 1], (8, RANK))
            if side == 0:
                t, spot = s, at
            else:
                t = 2 + 2 * s + side - 1
                spot = (at & 7) // 4 * (8 * nz) + (at // 8) * 8 + (at & 3)
                m.where[blocks_all * (t - 2) : blocks_all * (t - 1), :] = jnp.where(
                    block_id == jnp.broadcast_to(at[0:1, :], block_id.shape), 1.0, 0.0
                )
            spot = jnp.where(live, spot, -1000).astype(F32)
            spots = spots + jnp.where(lane == t, spot, 0.0)
    m.meta[...] = spots

    def prepare(slot, first, last):
        def one(t, carry):
            span = pl.ds(pl.multiple_of(t * RANK, RANK), RANK)
            part = m.xs[slot, :, span]
            top = part.astype(BF16)
            rest = part - top.astype(F32)
            m.xh[slot, :, span] = top
            m.xl[slot, :, span] = rest.astype(BF16)
            wide_top = top.astype(F32)
            turned = jnp.concatenate([wide_top, rest, wide_top], axis=0).T
            m.xt[slot, span, :] = turned.astype(BF16)
            return carry

        lax.fori_loop(first, last, one, 0)

    def pick_chunk(chunk):
        for b in range(4):
            held = m.full[pl.ds(pl.multiple_of(chunk * CHUNK + b * EDGE, EDGE), EDGE), :]
            for t in range(4):
                m.picks[EDGE * t : EDGE * t + EDGE, :] += (
                    m.where[pl.ds(blocks_all * t + chunk * 4 + b, 1), :] * held
                )

    loads[0].wait()
    m.full[pl.ds(pl.multiple_of(c * CHUNK, CHUNK), CHUNK), :] = m.mine[...]
    loads[3].wait()
    pieces = SPAN // RANK
    early = pieces // 2
    prepare(0, 0, early)
    pl.semaphore_wait(barrier, NX + NY + nz - 2)

    def piece_at(step, part, back):
        origin = (z + step) % nz if back else (z - step + nz) % nz
        return m.full.at[
            pl.ds(pl.multiple_of((origin * 2 + core) * CHUNK + part * SUB, SUB), SUB)
        ]

    def hop(step, part, back):
        peer = (z - 1 + nz) % nz if back else (z + 1) % nz
        src = m.mine.at[pl.ds(part * SUB, SUB)] if step == 0 else piece_at(step, part, back)
        return send(
            src,
            piece_at(step, part, back),
            "down" if back else "up",
            2 * step + part,
            narrow=peer * 2 + core,
        )

    across = []

    def to_partner(step, part, back):
        src = m.mine.at[pl.ds(part * SUB, SUB)] if step == 0 else piece_at(step, part, back)
        across.append(send(src, piece_at(step, part, back), "across", len(across), narrow=partner))

    half_way = nz // 2

    def parts_of(step, back):
        if step < half_way:
            return (0, 1)
        return (1,) if back else (0,)

    hops = {}
    for part in (0, 1):
        for back in (False, True):
            if part in parts_of(1, back):
                hops[1, part, back] = hop(0, part, back)
    meta_x = over_x("meta_sx", lambda peer: m.meta, m.meta_x, 8)
    m.meta_x[pl.ds(pl.multiple_of(x * 8, 8), 8), :] = m.meta[...]
    for part in (0, 1):
        to_partner(0, part, False)
    pick_chunk(c)
    own_chunk = m.mine[...]
    m.gram[...] = dot_full(own_chunk.T, own_chunk)
    jobs = [
        lambda: prepare(0, early, pieces),
        lambda: prepare(1, 0, pieces // 3),
        lambda: prepare(1, pieces // 3, pieces * 2 // 3),
        lambda: prepare(1, pieces * 2 // 3, pieces),
    ]

    def add_gram(origin):
        chunk = m.full[pl.ds(pl.multiple_of((origin * 2 + core) * CHUNK, CHUNK), CHUNK), :]
        m.gram[...] += dot_full(chunk.T, chunk)

    def pick_partner(step):
        first, last = (0, 2) if step == 0 else (4 * step - 2, min(4 * step + 2, 4 * half_way))
        arrived(across[first:last])
        pick_chunk((z + step) % nz * 2 + 1 - core)
        if 0 < step < half_way:
            pick_chunk((z - step + nz) % nz * 2 + 1 - core)

    meta_y = None
    for step in range(1, half_way + 1):
        for part in (0, 1):
            for back in (False, True):
                if part not in parts_of(step, back):
                    continue
                hops[step, part, back].wait_recv()
                if step < half_way and part in parts_of(step + 1, back):
                    hops[step + 1, part, back] = hop(step, part, back)
                to_partner(step, part, back)
        if step == 1:
            arrived(meta_x)
            for xx in range(NX):
                m.meta_row[xx : xx + 1, :] = m.meta_x[8 * xx : 8 * xx + 1, :]
            meta_y = over_y("meta_sy", lambda peer: m.meta_row, m.metas, 8)
            m.metas[pl.ds(pl.multiple_of(y * 8, 8), 8), :] = m.meta_row[...]
        add_gram((z + step) % nz)
        pick_chunk((z + step) % nz * 2 + core)
        if step < half_way:
            add_gram((z - step + nz) % nz)
            pick_chunk((z - step + nz) % nz * 2 + core)
        pick_partner(step - 1)
        if jobs:
            jobs.pop(0)()
    while jobs:
        jobs.pop(0)()

    grams = send(m.gram, m.gram_in, "grams", 0, narrow=partner)
    arrived(meta_y)
    places = jnp.concatenate([m.metas[8 * yy : 8 * yy + NX, :] for yy in range(NY)], axis=0)
    lanes = lax.broadcasted_iota(jnp.int32, (NW, RANK), 1).astype(F32)
    for t in range(6):
        place = jnp.broadcast_to(places[:, t : t + 1], (NW, RANK))
        for h in range(HALVES):
            if t < 2:
                hot = jnp.where(lanes == place + QB * h, 1.0, 0.0)
                m.pick_aux_t[pl.ds(2 * t + h, NW, stride=4), :] = hot
            else:
                side = (t - 2) % 2
                start = 4 * NW * ((t - 2) // 2) + 2 * side + h
                m.pick_orb_t[pl.ds(start, NW, stride=4), :] = jnp.where(
                    lanes == place + 4 * h, 1.0, 0.0
                )
    m.pick_aux[...] = m.pick_aux_t[...].T
    for s in range(2):
        m.pick_orb[s] = m.pick_orb_t[4 * NW * s : 4 * NW * (s + 1), :].T
    pick_partner(half_way)

    def block_rows(s, side):
        return m.picks[EDGE * (2 * s + side) : EDGE * (2 * s + side + 1), :]

    def eight_rows(s, t):
        return m.picks[pl.ds(pl.multiple_of(2 * EDGE * s + t * 8, 8), 8), :]

    for s in range(2):
        rows_j = block_rows(s, 1)

        def pairs(t, carry, s=s, rows_j=rows_j):
            span = pl.ds(pl.multiple_of(t * 512, 512), 512)
            both = (eight_rows(s, t)[:, None, :] * rows_j[None]).reshape(512, RANK)
            top = both.astype(BF16)
            m.krh[span, :] = top
            m.krl[span, :] = (both - top.astype(F32)).astype(BF16)
            return carry

        lax.fori_loop(0, 8, pairs, 0)
        m.terms[EDGE * s : EDGE * s + EDGE, :] = (
            dot_fast(m.xh[s], m.krh[...])
            + dot_fast(m.xh[s], m.krl[...])
            + dot_fast(m.xl[s], m.krh[...])
        )

    for s in range(2):
        for h in range(HALVES):
            m.fwd_rows[pl.ds(2 * s + h, NW, stride=4), :] = m.terms[
                EDGE * s + NW * h : EDGE * s + NW * (h + 1), :
            ]
    send_pieces("fwd_s", m.fwd_rows, m.fwd, m.fwd_in)

    grams.wait_recv()
    m.gram_b[...] = m.gram[...] + m.gram_in[...]
    m.inv[...] = m.gram_b[...] * m.gram_b[...]
    invert_steps(m.inv, 0, 16)
    take_pieces("fwd_s", m.fwd_in, m.fwd_rows)

    aux_sum = dot_full(m.pick_aux[0 : HALVES * QB, :], m.fwd_rows[...])
    aux_own = dot_full(aux_sum, m.inv[...])

    m.rep_rows[...] = dot_full(m.pick_aux_t[:, 0 : HALVES * QB], aux_own)
    send_pieces("rep_s", m.rep_rows, m.rep, m.rep_in)
    m.gram_own[...] = dot_full(aux_own.T, aux_own)
    send_pieces("tri_s", m.gram_own, m.tri, m.tri_in)

    to = lax.broadcasted_iota(jnp.int32, (NW, HALVES * QB), 0)
    what = lax.broadcasted_iota(jnp.int32, (NW, HALVES * QB), 1)
    target = (to % NY) * NX + to // NY
    share = jnp.where(what == target % 2 * QB + target // 2, 1.0, 0.0)
    m.own[...] = dot_full(share, aux_own)
    own_x = over_x("own_sx", lambda peer: rows_of(m.own, peer, NY), m.own_mid, NY)
    keep(m.own_mid, x, NY, m.own, x)

    arrived(own_x)
    m.own_turn[...] = jnp.zeros_like(m.own_turn)
    for xx in range(NX):
        m.own_turn[pl.ds(xx, NY, stride=8), :] = m.own_mid[NY * xx : NY * xx + NY, :]
    own_y = over_y("own_sy", lambda peer: rows_of(m.own_turn, peer, 8), m.own_in, 8)
    keep(m.own_in, y, 8, m.own_turn, y)

    take_pieces("rep_s", m.rep_in, m.rep_rows)

    for s in range(2):
        aux_rows = jnp.concatenate(
            [m.rep_rows[pl.ds(2 * s + h, NW, stride=4), :] for h in range(HALVES)], axis=0
        )
        top = aux_rows.astype(BF16)
        rest = (aux_rows - top.astype(F32)).astype(BF16)
        stacked = jnp.concatenate([top, top, rest], axis=0)
        rows_j = block_rows(s, 1)

        m.spread[...] = dot_fast(m.xt[s], stacked)

        def sums(t, term_j, s=s, rows_j=rows_j):
            for k in range(8):
                i = t * 8 + k
                part = m.spread[pl.ds(pl.multiple_of(i * EDGE, EDGE), EDGE), :]
                m.terms[pl.ds(2 * EDGE * s + i, 1), :] = jnp.sum(
                    part * rows_j, axis=0, keepdims=True
                )
                term_j = term_j + part * m.picks[pl.ds(2 * EDGE * s + i, 1), :]
            return term_j

        term_j = lax.fori_loop(0, 8, sums, jnp.zeros((EDGE, RANK), F32))
        m.terms[EDGE * (2 * s + 1) : EDGE * (2 * s + 2), :] = term_j
        for side in range(2):
            for h in range(HALVES):
                start = EDGE * (2 * s + side) + NW * h
                m.orb_rows[pl.ds(2 * side + h, NW, stride=4), :] = m.terms[start : start + NW, :]
        if s == 0:
            send_pieces("orb_0", m.orb_rows, m.orb_0, m.orb_in_0)
            all_in("tri_s", m.tri_in.at[pl.ds(0, NW - 1)])
            total = m.tri_in[0]
            for k in range(1, NW):
                total = total + m.tri_in[k]
            m.tile[4:8, :] = total
            tile_core = send(m.tile, m.tile_core, "tile_sc", 0, narrow=partner)
        else:
            send_pieces("orb_1", m.orb_rows, m.orb_1, m.orb_in_1)
    tile_core.wait_recv()
    m.tile_sum[...] = m.tile[...] + m.tile_core[...]
    tile_z = over_z("tile_sz", lambda peer: m.tile_sum, m.tile_z, 8)
    m.tile_z[pl.ds(pl.multiple_of(z * 8, 8), 8), :] = m.tile_sum[...]

    arrived(own_y)
    for yy in range(NY):
        aux_out[NX * yy : NX * yy + NX, :] = m.own_in[8 * yy : 8 * yy + NX, :]

    arrived(tile_z)
    total = m.tile_z[0:8, :]
    for k in range(1, nz):
        total = total + m.tile_z[8 * k : 8 * k + 8, :]
    m.tile_all[...] = total
    tile_y = over_y("tile_sy", lambda peer: m.tile_all, m.tile_y, 8)
    m.tile_y[pl.ds(pl.multiple_of(y * 8, 8), 8), :] = total

    take_pieces("orb_0", m.orb_in_0, m.got_rows)
    m.dense[...] = dot_full(m.pick_orb[0, 0 : 16 * nz, :], m.got_rows[...])
    take_pieces("orb_1", m.orb_in_1, m.got_rows)
    m.dense[...] = m.dense[...] + dot_full(m.pick_orb[1, 0 : 16 * nz, :], m.got_rows[...])
    size = 8 * nz
    dense_core = send(rows_of(m.dense, 1 - core, size), m.dense_core, "dense_sc", 0, narrow=partner)
    dense_core.wait_recv()
    m.part[...] = m.dense[pl.ds(pl.multiple_of(core * size, 8), size), :] + m.dense_core[...]
    part_z = over_z("part_sz", lambda peer: rows_of(m.part, peer, 8), m.part_z, 8)
    keep(m.part_z, z, 8, m.part, z)

    arrived(tile_y)
    size = 8 * NY
    tile_x = over_x("tile_sx", lambda peer: m.tile_y, m.tile_x, size)
    m.tile_x[pl.ds(pl.multiple_of(x * size, 8), size), :] = m.tile_y[...]

    arrived(part_z)
    total = m.part_z[0:8, :]
    for k in range(1, nz):
        total = total + m.part_z[8 * k : 8 * k + 8, :]
    m.sum_own[...] = total
    sum_y = over_y("sum_sy", lambda peer: m.sum_own, m.sum_y, 8)
    m.sum_y[pl.ds(pl.multiple_of(y * 8, 8), 8), :] = total

    arrived(tile_x)
    for xx in range(NX):
        for yy in range(NY):
            at, to_row = 8 * (xx * NY + yy) + 4, 4 * (yy * NX + xx)
            m.gram_a[to_row : to_row + 4, :] = m.tile_x[at : at + 4, :]
    m.inv[...] = 2.0 * m.gram_a[...] * m.gram_b[...]
    invert_steps(m.inv, 0, 8)
    arrived(sum_y)
    size = 8 * NY
    sum_x = over_x("sum_sx", lambda peer: m.sum_y, m.sum_x, size)
    m.sum_x[pl.ds(pl.multiple_of(x * size, 8), size), :] = m.sum_y[...]
    invert_steps(m.inv, 8, 16)
    arrived(sum_x)
    m.final[...] = dot_full(m.sum_x[...], m.inv[...])
    for xx in range(NX):
        for b in range(4):
            for h in range(HALVES):
                orb_out[pl.ds(EDGE * b + NW * h + xx, NY, stride=NX), :] = m.final[
                    pl.ds(8 * NY * xx + 4 * h + b, NY, stride=8), :
                ]
    for copy in pending:
        copy.wait_send()
    for name, pieces in (
        ("fwd_s", m.fwd),
        ("rep_s", m.rep),
        ("tri_s", m.tri),
        ("orb_0", m.orb_0),
        ("orb_1", m.orb_1),
    ):
        all_in(name, pieces.at[pl.ds(0, NW - 1)], sent)


def on_device(blocks, block_coords, block_count, orbital_factor, *, nz):
    vmem, sems = scratch_plan(nz)
    scratch = [pltpu.VMEM(shape, dtype) for shape, dtype in vmem.values()]
    scratch += [pltpu.SemaphoreType.DMA((n,)) for n in sems.values()] * 2
    aux, orbital = pl.pallas_call(
        functools.partial(kernel, nz),
        out_shape=(
            jax.ShapeDtypeStruct((NW, RANK), F32),
            jax.ShapeDtypeStruct((CHUNK, RANK), F32),
        ),
        in_specs=[
            pl.BlockSpec(memory_space=pl.ANY),
            pl.BlockSpec(memory_space=pl.ANY),
            pl.BlockSpec(memory_space=pl.ANY),
            pl.BlockSpec(memory_space=pl.ANY),
        ],
        out_specs=(
            pl.BlockSpec(memory_space=pltpu.VMEM),
            pl.BlockSpec(memory_space=pltpu.VMEM),
        ),
        scratch_shapes=scratch,
        compiler_params=pltpu.CompilerParams(
            collective_id=0, has_side_effects=True, vmem_limit_bytes=67_043_328 - (160 << 10)
        ),
    )(
        block_coords.reshape(2, 3),
        block_count.reshape(1, 1),
        orbital_factor,
        blocks.reshape(2, EDGE, SPAN),
    )
    return aux[None], orbital


def solution(mesh):
    return jax.shard_map(
        functools.partial(on_device, nz=mesh.shape["narrow"] // 2),
        mesh=mesh,
        in_specs=(
            P("wide", "narrow", None, None, None),
            P("wide", "narrow", None, None),
            P("wide", "narrow"),
            P("narrow", None),
        ),
        out_specs=(P("narrow", "wide", None), P("narrow", None)),
        check_vma=False,
    )
```

```python
import functools
import types

import jax
import jax.numpy as jnp
from jax import lax
from jax.experimental import pallas as pl
from jax.experimental.pallas import tpu as pltpu
from jax.sharding import PartitionSpec as P

NX, NY = 4, 8
NW = NX * NY
EDGE = 64
RANK = 128
HALVES = EDGE // NW
QB = 16
SPAN = EDGE * EDGE
CHUNK = 256
PARTS = 4
SUB = CHUNK // PARTS
F32, BF16 = jnp.float32, jnp.bfloat16
HIGHEST = lax.Precision.HIGHEST


def dot_full(left, right):
    return jnp.dot(left, right, precision=HIGHEST, preferred_element_type=F32)


def dot_fast(left, right):
    return jnp.dot(left, right, preferred_element_type=F32)


def pivot_step(rows):
    lane = lax.broadcasted_iota(jnp.int32, (8, RANK), 1)
    sub = lax.broadcasted_iota(jnp.int32, (8, RANK), 0)
    head = lane < 8

    def over_lanes(block, column):
        return jnp.broadcast_to(block[:, column : column + 1], (8, RANK))

    def over_rows(block, row):
        return jnp.broadcast_to(block[row : row + 1, :], (8, RANK))

    panel = rows[0]
    cols = [over_lanes(panel, m) for m in range(8)]
    for j in range(8):
        scale = 1.0 / over_rows(cols[j], j)
        fresh = []
        for m in range(8):
            if m == j:
                fresh.append(jnp.where(sub == j, scale, -cols[j] * scale))
            else:
                ratio = over_rows(cols[m], j) * scale
                fresh.append(jnp.where(sub == j, ratio, cols[m] - cols[j] * ratio))
        cols = fresh
    panel = jnp.where(head, jnp.where(lane == sub, 1.0, 0.0), panel)
    solved = cols[0] * over_rows(panel, 0)
    for m in range(1, 8):
        solved = solved + cols[m] * over_rows(panel, m)
    spread = [over_rows(solved, m) for m in range(8)]
    out = []
    for row in rows[1:]:
        total = jnp.where(head, 0.0, row)
        for m in range(8):
            total = total - over_lanes(row, m) * spread[m]
        out.append(total)
    out.append(solved)
    return tuple(pltpu.roll(block, RANK - 8, 1) for block in out)


def invert_steps(ref, first, last):
    rows = tuple(ref[8 * k : 8 * k + 8, :] for k in range(16))
    rows = lax.fori_loop(first, last, lambda t, held: pivot_step(held), rows)
    for k in range(16):
        ref[8 * k : 8 * k + 8, :] = rows[k]


def scratch_plan(nz):
    nc = 2 * nz
    vmem = dict(
        xs=((2, EDGE, SPAN), F32),
        xh=((2, EDGE, SPAN), BF16),
        xl=((2, EDGE, SPAN), BF16),
        xt=((2, SPAN, 3 * EDGE), BF16),
        full=((CHUNK * nc, RANK), F32),
        where=((4 * 8 * nz, RANK), F32),
        picks=((4 * EDGE, RANK), F32),
        krh=((SPAN, RANK), BF16),
        krl=((SPAN, RANK), BF16),
        gram=((RANK, RANK), F32),
        gram_in=((RANK, RANK), F32),
        gram_b=((RANK, RANK), F32),
        gram_own=((RANK, RANK), F32),
        gram_a=((RANK, RANK), F32),
        inv=((RANK, RANK), F32),
        where_at=((2, 3), jnp.int32),
        lived=((1, 1), jnp.int32),
        mine=((CHUNK, RANK), F32),
        meta=((8, RANK), F32),
        meta_x=((8 * NX, RANK), F32),
        meta_row=((8, RANK), F32),
        metas=((8 * NY, RANK), F32),
        spread=((SPAN, RANK), F32),
        pick_aux_t=((4 * NW, RANK), F32),
        pick_aux=((RANK, 4 * NW), F32),
        pick_orb_t=((8 * NW, RANK), F32),
        pick_orb=((2, RANK, 4 * NW), F32),
        terms=((4 * EDGE, RANK), F32),
        fwd=((NW, 4, RANK), F32),
        fwd_in=((NW, 4, RANK), F32),
        fwd_rows=((4 * NW, RANK), F32),
        rep=((NW, 4, RANK), F32),
        rep_in=((NW, 4, RANK), F32),
        rep_rows=((4 * NW, RANK), F32),
        tri=((NW, 4, RANK), F32),
        tri_in=((NW, 4, RANK), F32),
        own=((NW, RANK), F32),
        own_mid=((NW, RANK), F32),
        own_turn=((8 * NY, RANK), F32),
        own_in=((8 * NY, RANK), F32),
        tile=((8, RANK), F32),
        tile_core=((8, RANK), F32),
        tile_sum=((8, RANK), F32),
        tile_all=((8, RANK), F32),
        sum_own=((8, RANK), F32),
        tile_z=((8 * nz, RANK), F32),
        tile_y=((8 * NY, RANK), F32),
        tile_x=((8 * NW, RANK), F32),
        orb_0=((NW, 4, RANK), F32),
        orb_1=((NW, 4, RANK), F32),
        orb_in_0=((NW, 4, RANK), F32),
        orb_in_1=((NW, 4, RANK), F32),
        orb_rows=((4 * NW, RANK), F32),
        got_rows=((4 * NW, RANK), F32),
        dense=((16 * nz, RANK), F32),
        dense_core=((8 * nz, RANK), F32),
        part=((8 * nz, RANK), F32),
        part_z=((8 * nz, RANK), F32),
        sum_y=((8 * NY, RANK), F32),
        sum_x=((8 * NW, RANK), F32),
        final=((8 * NW, RANK), F32),
    )
    sems = dict(
        load=4,
        up=PARTS * nz // 2,
        down=PARTS * nz // 2,
        across=PARTS * nz,
        grams=1,
        meta_sx=NX,
        meta_sy=NY,
        fwd_s=1,
        rep_s=1,
        tri_s=1,
        own_sx=NX,
        own_sy=NY,
        tile_sc=1,
        tile_sz=nz,
        tile_sy=NY,
        tile_sx=NX,
        orb_0=1,
        orb_1=1,
        dense_sc=1,
        part_sz=nz,
        sum_sy=NY,
        sum_sx=NX,
    )
    return vmem, sems


def kernel(nz, coords, count, b_in, blocks, aux_out, orb_out, *scratch):
    vmem, sems = scratch_plan(nz)
    m = types.SimpleNamespace(**dict(zip(vmem, scratch)))
    rest = scratch[len(vmem) :]
    sent = dict(zip(sems, rest[: len(sems)]))
    got = dict(zip(sems, rest[len(sems) :]))

    w = lax.axis_index("wide")
    c = lax.axis_index("narrow")
    x, y = w % NX, w // NX
    z, core = c // 2, c % 2
    pending = []

    def send(src, dst, name, index, wide=None, narrow=None):
        copy = pltpu.make_async_remote_copy(
            src_ref=src,
            dst_ref=dst,
            send_sem=sent[name].at[index],
            recv_sem=got[name].at[index],
            device_id=(w if wide is None else wide, c if narrow is None else narrow),
            device_id_type=pl.DeviceIdType.MESH,
        )
        copy.start()
        pending.append(copy)
        return copy

    def rows_of(ref, index, size):
        return ref.at[pl.ds(pl.multiple_of(index * size, 8), size)]

    def over_x(name, piece, dst, size):
        copies = []
        for d in range(1, NX):
            peer = (x + d) % NX
            copies.append(send(piece(peer), rows_of(dst, x, size), name, d, wide=y * NX + peer))
        return copies

    def over_y(name, piece, dst, size):
        copies = []
        for d in range(1, NY):
            peer = (y + d) % NY
            copies.append(send(piece(peer), rows_of(dst, y, size), name, d, wide=peer * NX + x))
        return copies

    def over_z(name, piece, dst, size):
        copies = []
        for d in range(1, nz):
            peer = (z + d) % nz
            copies.append(send(piece(peer), rows_of(dst, z, size), name, d, narrow=peer * 2 + core))
        return copies

    def to_all(name, src_of, dst):
        for dy in sorted(range(NY), key=lambda d: -min(d, NY - d)):
            for dx in sorted(range(NX), key=lambda d: -min(d, NX - d)):
                if dx or dy:
                    peer = (y + dy) % NY * NX + (x + dx) % NX
                    pltpu.make_async_remote_copy(
                        src_ref=src_of(peer),
                        dst_ref=dst,
                        send_sem=sent[name].at[0],
                        recv_sem=got[name].at[0],
                        device_id=(peer, c),
                        device_id_type=pl.DeviceIdType.MESH,
                    ).start()

    def send_pieces(name, rows, pieces, into):
        for k in range(NW):
            pieces[k] = rows[4 * k : 4 * k + 4, :]
        to_all(name, lambda peer: pieces.at[peer], into.at[w])
        into[w] = pieces[w]

    def take_pieces(name, into, rows):
        all_in(name, into.at[pl.ds(0, NW - 1)])
        for k in range(NW):
            rows[4 * k : 4 * k + 4, :] = into[k]

    def all_in(name, others, which=None):
        sem = (got if which is None else which)[name].at[0]
        pltpu.make_async_copy(others, others, sem).wait()

    def arrived(copies):
        for copy in copies:
            copy.wait_recv()

    def keep(dst, index, size, src, src_index):
        dst[pl.ds(pl.multiple_of(index * size, 8), size), :] = src[
            pl.ds(pl.multiple_of(src_index * size, 8), size), :
        ]

    loads = [
        pltpu.make_async_copy(src, dst, sent["load"].at[k])
        for k, (src, dst) in enumerate(
            [(b_in, m.mine), (coords, m.where_at), (count, m.lived), (blocks, m.xs)]
        )
    ]
    for copy in loads:
        copy.start()

    barrier = pltpu.get_barrier_semaphore()
    for d in range(1, NX):
        pl.semaphore_signal(
            barrier, inc=1, device_id=(y * NX + (x + d) % NX, c), device_id_type=pl.DeviceIdType.MESH
        )
    for d in range(1, NY):
        pl.semaphore_signal(
            barrier, inc=1, device_id=((y + d) % NY * NX + x, c), device_id_type=pl.DeviceIdType.MESH
        )
    for d in range(1, nz):
        pl.semaphore_signal(
            barrier, inc=1, device_id=(w, (z + d) % nz * 2 + core), device_id_type=pl.DeviceIdType.MESH
        )
    partner = z * 2 + 1 - core
    pl.semaphore_signal(barrier, inc=1, device_id=(w, partner), device_id_type=pl.DeviceIdType.MESH)

    m.picks[...] = jnp.zeros_like(m.picks)
    m.tile[...] = jnp.zeros_like(m.tile)
    m.meta_row[...] = jnp.zeros_like(m.meta_row)

    loads[1].wait()
    loads[2].wait()
    lane = lax.broadcasted_iota(jnp.int32, (8, RANK), 1)
    blocks_all = 8 * nz
    block_id = lax.broadcasted_iota(jnp.int32, (blocks_all, RANK), 0)
    spots = jnp.zeros((8, RANK), F32)
    for s in range(2):
        live = jnp.broadcast_to(m.lived[0:1, 0:1], (8, RANK)) > s
        for side in range(3):
            at = jnp.broadcast_to(m.where_at[s : s + 1, side : side + 1], (8, RANK))
            if side == 0:
                t, spot = s, at
            else:
                t = 2 + 2 * s + side - 1
                spot = (at & 7) // 4 * (8 * nz) + (at // 8) * 8 + (at & 3)
                m.where[blocks_all * (t - 2) : blocks_all * (t - 1), :] = jnp.where(
                    block_id == jnp.broadcast_to(at[0:1, :], block_id.shape), 1.0, 0.0
                )
            spot = jnp.where(live, spot, -1000).astype(F32)
            spots = spots + jnp.where(lane == t, spot, 0.0)
    m.meta[...] = spots

    def prepare(slot, first, last):
        def one(t, carry):
            span = pl.ds(pl.multiple_of(t * RANK, RANK), RANK)
            part = m.xs[slot, :, span]
            top = part.astype(BF16)
            rest = part - top.astype(F32)
            m.xh[slot, :, span] = top
            m.xl[slot, :, span] = rest.astype(BF16)
            wide_top = top.astype(F32)
            turned = jnp.concatenate([wide_top, rest, wide_top], axis=0).T
            m.xt[slot, span, :] = turned.astype(BF16)
            return carry

        lax.fori_loop(first, last, one, 0)

    def pick_chunk(chunk):
        for b in range(4):
            held = m.full[pl.ds(pl.multiple_of(chunk * CHUNK + b * EDGE, EDGE), EDGE), :]
            for t in range(4):
                m.picks[EDGE * t : EDGE * t + EDGE, :] += (
                    m.where[pl.ds(blocks_all * t + chunk * 4 + b, 1), :] * held
                )

    loads[0].wait()
    m.full[pl.ds(pl.multiple_of(c * CHUNK, CHUNK), CHUNK), :] = m.mine[...]
    loads[3].wait()
    pieces = SPAN // RANK
    early = pieces // 2
    prepare(0, 0, early)
    pl.semaphore_wait(barrier, NX + NY + nz - 2)

    def piece_at(step, part, back):
        origin = (z + step) % nz if back else (z - step + nz) % nz
        return m.full.at[
            pl.ds(pl.multiple_of((origin * 2 + core) * CHUNK + part * SUB, SUB), SUB)
        ]

    def hop(step, part, back):
        peer = (z - 1 + nz) % nz if back else (z + 1) % nz
        src = m.mine.at[pl.ds(part * SUB, SUB)] if step == 0 else piece_at(step, part, back)
        return send(
            src,
            piece_at(step, part, back),
            "down" if back else "up",
            PARTS * step + part,
            narrow=peer * 2 + core,
        )

    across = []

    def to_partner(step, part, back):
        src = m.mine.at[pl.ds(part * SUB, SUB)] if step == 0 else piece_at(step, part, back)
        across.append(send(src, piece_at(step, part, back), "across", len(across), narrow=partner))

    half_way = nz // 2

    def parts_of(step, back):
        if step < half_way:
            return range(PARTS)
        return range(PARTS // 2, PARTS) if back else range(PARTS // 2)

    hops = {}
    for part in range(PARTS):
        for back in (False, True):
            if part in parts_of(1, back):
                hops[1, part, back] = hop(0, part, back)
    meta_x = over_x("meta_sx", lambda peer: m.meta, m.meta_x, 8)
    m.meta_x[pl.ds(pl.multiple_of(x * 8, 8), 8), :] = m.meta[...]
    for part in range(PARTS):
        to_partner(0, part, False)
    pick_chunk(c)
    own_chunk = m.mine[...]
    m.gram[...] = dot_full(own_chunk.T, own_chunk)
    jobs = [
        lambda: prepare(0, early, pieces),
        lambda: prepare(1, 0, pieces // 3),
        lambda: prepare(1, pieces // 3, pieces * 2 // 3),
        lambda: prepare(1, pieces * 2 // 3, pieces),
    ]

    def add_gram(origin):
        chunk = m.full[pl.ds(pl.multiple_of((origin * 2 + core) * CHUNK, CHUNK), CHUNK), :]
        m.gram[...] += dot_full(chunk.T, chunk)

    def pick_partner(step):
        first = 0 if step == 0 else PARTS * (2 * step - 1)
        last = min(PARTS * (2 * step + 1), PARTS * nz)
        arrived(across[first:last])
        pick_chunk((z + step) % nz * 2 + 1 - core)
        if 0 < step < half_way:
            pick_chunk((z - step + nz) % nz * 2 + 1 - core)

    meta_y = None
    for step in range(1, half_way + 1):
        for part in range(PARTS):
            for back in (False, True):
                if part not in parts_of(step, back):
                    continue
                hops[step, part, back].wait_recv()
                if step < half_way and part in parts_of(step + 1, back):
                    hops[step + 1, part, back] = hop(step, part, back)
                to_partner(step, part, back)
        if step == 1:
            arrived(meta_x)
            for xx in range(NX):
                m.meta_row[xx : xx + 1, :] = m.meta_x[8 * xx : 8 * xx + 1, :]
            meta_y = over_y("meta_sy", lambda peer: m.meta_row, m.metas, 8)
            m.metas[pl.ds(pl.multiple_of(y * 8, 8), 8), :] = m.meta_row[...]
        add_gram((z + step) % nz)
        pick_chunk((z + step) % nz * 2 + core)
        if step < half_way:
            add_gram((z - step + nz) % nz)
            pick_chunk((z - step + nz) % nz * 2 + core)
        pick_partner(step - 1)
        if jobs:
            jobs.pop(0)()
    while jobs:
        jobs.pop(0)()

    grams = send(m.gram, m.gram_in, "grams", 0, narrow=partner)
    arrived(meta_y)
    places = jnp.concatenate([m.metas[8 * yy : 8 * yy + NX, :] for yy in range(NY)], axis=0)
    lanes = lax.broadcasted_iota(jnp.int32, (NW, RANK), 1).astype(F32)
    for t in range(6):
        place = jnp.broadcast_to(places[:, t : t + 1], (NW, RANK))
        for h in range(HALVES):
            if t < 2:
                hot = jnp.where(lanes == place + QB * h, 1.0, 0.0)
                m.pick_aux_t[pl.ds(2 * t + h, NW, stride=4), :] = hot
            else:
                side = (t - 2) % 2
                start = 4 * NW * ((t - 2) // 2) + 2 * side + h
                m.pick_orb_t[pl.ds(start, NW, stride=4), :] = jnp.where(
                    lanes == place + 4 * h, 1.0, 0.0
                )
    m.pick_aux[...] = m.pick_aux_t[...].T
    for s in range(2):
        m.pick_orb[s] = m.pick_orb_t[4 * NW * s : 4 * NW * (s + 1), :].T
    pick_partner(half_way)

    def block_rows(s, side):
        return m.picks[EDGE * (2 * s + side) : EDGE * (2 * s + side + 1), :]

    def eight_rows(s, t):
        return m.picks[pl.ds(pl.multiple_of(2 * EDGE * s + t * 8, 8), 8), :]

    for s in range(2):
        rows_j = block_rows(s, 1)

        def pairs(t, carry, s=s, rows_j=rows_j):
            span = pl.ds(pl.multiple_of(t * 512, 512), 512)
            both = (eight_rows(s, t)[:, None, :] * rows_j[None]).reshape(512, RANK)
            top = both.astype(BF16)
            m.krh[span, :] = top
            m.krl[span, :] = (both - top.astype(F32)).astype(BF16)
            return carry

        lax.fori_loop(0, 8, pairs, 0)
        m.terms[EDGE * s : EDGE * s + EDGE, :] = (
            dot_fast(m.xh[s], m.krh[...])
            + dot_fast(m.xh[s], m.krl[...])
            + dot_fast(m.xl[s], m.krh[...])
        )

    for s in range(2):
        for h in range(HALVES):
            m.fwd_rows[pl.ds(2 * s + h, NW, stride=4), :] = m.terms[
                EDGE * s + NW * h : EDGE * s + NW * (h + 1), :
            ]
    send_pieces("fwd_s", m.fwd_rows, m.fwd, m.fwd_in)

    grams.wait_recv()
    m.gram_b[...] = m.gram[...] + m.gram_in[...]
    m.inv[...] = m.gram_b[...] * m.gram_b[...]
    invert_steps(m.inv, 0, 16)
    take_pieces("fwd_s", m.fwd_in, m.fwd_rows)

    aux_sum = dot_full(m.pick_aux[0 : HALVES * QB, :], m.fwd_rows[...])
    aux_own = dot_full(aux_sum, m.inv[...])

    m.rep_rows[...] = dot_full(m.pick_aux_t[:, 0 : HALVES * QB], aux_own)
    send_pieces("rep_s", m.rep_rows, m.rep, m.rep_in)
    m.gram_own[...] = dot_full(aux_own.T, aux_own)
    send_pieces("tri_s", m.gram_own, m.tri, m.tri_in)

    to = lax.broadcasted_iota(jnp.int32, (NW, HALVES * QB), 0)
    what = lax.broadcasted_iota(jnp.int32, (NW, HALVES * QB), 1)
    target = (to % NY) * NX + to // NY
    share = jnp.where(what == target % 2 * QB + target // 2, 1.0, 0.0)
    m.own[...] = dot_full(share, aux_own)
    own_x = over_x("own_sx", lambda peer: rows_of(m.own, peer, NY), m.own_mid, NY)
    keep(m.own_mid, x, NY, m.own, x)

    arrived(own_x)
    m.own_turn[...] = jnp.zeros_like(m.own_turn)
    for xx in range(NX):
        m.own_turn[pl.ds(xx, NY, stride=8), :] = m.own_mid[NY * xx : NY * xx + NY, :]
    own_y = over_y("own_sy", lambda peer: rows_of(m.own_turn, peer, 8), m.own_in, 8)
    keep(m.own_in, y, 8, m.own_turn, y)

    take_pieces("rep_s", m.rep_in, m.rep_rows)

    for s in range(2):
        aux_rows = jnp.concatenate(
            [m.rep_rows[pl.ds(2 * s + h, NW, stride=4), :] for h in range(HALVES)], axis=0
        )
        top = aux_rows.astype(BF16)
        rest = (aux_rows - top.astype(F32)).astype(BF16)
        stacked = jnp.concatenate([top, top, rest], axis=0)
        rows_j = block_rows(s, 1)

        m.spread[...] = dot_fast(m.xt[s], stacked)

        def sums(t, term_j, s=s, rows_j=rows_j):
            for k in range(8):
                i = t * 8 + k
                part = m.spread[pl.ds(pl.multiple_of(i * EDGE, EDGE), EDGE), :]
                m.terms[pl.ds(2 * EDGE * s + i, 1), :] = jnp.sum(
                    part * rows_j, axis=0, keepdims=True
                )
                term_j = term_j + part * m.picks[pl.ds(2 * EDGE * s + i, 1), :]
            return term_j

        term_j = lax.fori_loop(0, 8, sums, jnp.zeros((EDGE, RANK), F32))
        m.terms[EDGE * (2 * s + 1) : EDGE * (2 * s + 2), :] = term_j
        for side in range(2):
            for h in range(HALVES):
                start = EDGE * (2 * s + side) + NW * h
                m.orb_rows[pl.ds(2 * side + h, NW, stride=4), :] = m.terms[start : start + NW, :]
        if s == 0:
            send_pieces("orb_0", m.orb_rows, m.orb_0, m.orb_in_0)
            all_in("tri_s", m.tri_in.at[pl.ds(0, NW - 1)])
            total = m.tri_in[0]
            for k in range(1, NW):
                total = total + m.tri_in[k]
            m.tile[4:8, :] = total
            tile_core = send(m.tile, m.tile_core, "tile_sc", 0, narrow=partner)
        else:
            send_pieces("orb_1", m.orb_rows, m.orb_1, m.orb_in_1)
    tile_core.wait_recv()
    m.tile_sum[...] = m.tile[...] + m.tile_core[...]
    tile_z = over_z("tile_sz", lambda peer: m.tile_sum, m.tile_z, 8)
    m.tile_z[pl.ds(pl.multiple_of(z * 8, 8), 8), :] = m.tile_sum[...]

    arrived(own_y)
    for yy in range(NY):
        aux_out[NX * yy : NX * yy + NX, :] = m.own_in[8 * yy : 8 * yy + NX, :]

    arrived(tile_z)
    total = m.tile_z[0:8, :]
    for k in range(1, nz):
        total = total + m.tile_z[8 * k : 8 * k + 8, :]
    m.tile_all[...] = total
    tile_y = over_y("tile_sy", lambda peer: m.tile_all, m.tile_y, 8)
    m.tile_y[pl.ds(pl.multiple_of(y * 8, 8), 8), :] = total

    take_pieces("orb_0", m.orb_in_0, m.got_rows)
    m.dense[...] = dot_full(m.pick_orb[0, 0 : 16 * nz, :], m.got_rows[...])
    take_pieces("orb_1", m.orb_in_1, m.got_rows)
    m.dense[...] = m.dense[...] + dot_full(m.pick_orb[1, 0 : 16 * nz, :], m.got_rows[...])
    size = 8 * nz
    dense_core = send(rows_of(m.dense, 1 - core, size), m.dense_core, "dense_sc", 0, narrow=partner)
    dense_core.wait_recv()
    m.part[...] = m.dense[pl.ds(pl.multiple_of(core * size, 8), size), :] + m.dense_core[...]
    part_z = over_z("part_sz", lambda peer: rows_of(m.part, peer, 8), m.part_z, 8)
    keep(m.part_z, z, 8, m.part, z)

    arrived(tile_y)
    size = 8 * NY
    tile_x = over_x("tile_sx", lambda peer: m.tile_y, m.tile_x, size)
    m.tile_x[pl.ds(pl.multiple_of(x * size, 8), size), :] = m.tile_y[...]

    arrived(part_z)
    total = m.part_z[0:8, :]
    for k in range(1, nz):
        total = total + m.part_z[8 * k : 8 * k + 8, :]
    m.sum_own[...] = total
    sum_y = over_y("sum_sy", lambda peer: m.sum_own, m.sum_y, 8)
    m.sum_y[pl.ds(pl.multiple_of(y * 8, 8), 8), :] = total

    arrived(tile_x)
    for xx in range(NX):
        for yy in range(NY):
            at, to_row = 8 * (xx * NY + yy) + 4, 4 * (yy * NX + xx)
            m.gram_a[to_row : to_row + 4, :] = m.tile_x[at : at + 4, :]
    m.inv[...] = 2.0 * m.gram_a[...] * m.gram_b[...]
    invert_steps(m.inv, 0, 8)
    arrived(sum_y)
    size = 8 * NY
    sum_x = over_x("sum_sx", lambda peer: m.sum_y, m.sum_x, size)
    m.sum_x[pl.ds(pl.multiple_of(x * size, 8), size), :] = m.sum_y[...]
    invert_steps(m.inv, 8, 16)
    arrived(sum_x)
    m.final[...] = dot_full(m.sum_x[...], m.inv[...])
    for xx in range(NX):
        for b in range(4):
            for h in range(HALVES):
                orb_out[pl.ds(EDGE * b + NW * h + xx, NY, stride=NX), :] = m.final[
                    pl.ds(8 * NY * xx + 4 * h + b, NY, stride=8), :
                ]
    for copy in pending:
        copy.wait_send()
    for name, pieces in (
        ("fwd_s", m.fwd),
        ("rep_s", m.rep),
        ("tri_s", m.tri),
        ("orb_0", m.orb_0),
        ("orb_1", m.orb_1),
    ):
        all_in(name, pieces.at[pl.ds(0, NW - 1)], sent)


def on_device(blocks, block_coords, block_count, orbital_factor, *, nz):
    vmem, sems = scratch_plan(nz)
    scratch = [pltpu.VMEM(shape, dtype) for shape, dtype in vmem.values()]
    scratch += [pltpu.SemaphoreType.DMA((n,)) for n in sems.values()] * 2
    aux, orbital = pl.pallas_call(
        functools.partial(kernel, nz),
        out_shape=(
            jax.ShapeDtypeStruct((NW, RANK), F32),
            jax.ShapeDtypeStruct((CHUNK, RANK), F32),
        ),
        in_specs=[
            pl.BlockSpec(memory_space=pl.ANY),
            pl.BlockSpec(memory_space=pl.ANY),
            pl.BlockSpec(memory_space=pl.ANY),
            pl.BlockSpec(memory_space=pl.ANY),
        ],
        out_specs=(
            pl.BlockSpec(memory_space=pltpu.VMEM),
            pl.BlockSpec(memory_space=pltpu.VMEM),
        ),
        scratch_shapes=scratch,
        compiler_params=pltpu.CompilerParams(
            collective_id=0, has_side_effects=True, vmem_limit_bytes=(54 << 20) - (240 << 10)
        ),
    )(
        block_coords.reshape(2, 3),
        block_count.reshape(1, 1),
        orbital_factor,
        blocks.reshape(2, EDGE, SPAN),
    )
    return aux[None], orbital


def solution(mesh):
    return jax.shard_map(
        functools.partial(on_device, nz=mesh.shape["narrow"] // 2),
        mesh=mesh,
        in_specs=(
            P("wide", "narrow", None, None, None),
            P("wide", "narrow", None, None),
            P("wide", "narrow"),
            P("narrow", None),
        ),
        out_specs=(P("narrow", "wide", None), P("narrow", None)),
        check_vma=False,
    )
```
